32 devices in a mesh: sp: 8 (over z, x), rep: 4 (over y, core).
Axes of the slice: x: 2, y: 2, z: 4, core: 2. Of those that a mesh axis runs over, the one named last changes fastest.
Arguments:
- incoming_embeddings: bfloat16 [4, 16, 256, 512], P('rep', 'sp'), may hold values from -16 to 16
- output_sensitivity: bfloat16 [4, 16, 256, 512], P('rep', 'sp'), may hold values from -6 to 6
- mixing_prenormal_multiplier: float32 [512], replicated, may hold values from 0.5 to 1.5
- triple_mapping_matrix: bfloat16 [512, 1536], replicated, may hold values from -1 to 1
- head_sharpness: float32 [8], replicated, may hold values from 0.5 to 300
- output_mapping_matrix: bfloat16 [512, 512], replicated, may hold values from -0.25 to 0.25
- residual_arm_factors: float32 [2, 512], replicated, may hold values from 0.5 to 1.5
- locality_prenormal_multiplier: float32 [512], replicated, may hold values from 0.5 to 1.5
- separable_kernel_pair: float32 [2, 3, 3, 512], replicated, may hold values from -2 to 2
Outputs:
- grad_input: bfloat16 [4, 16, 256, 512], P('rep', 'sp')
- grad_qkv: float32 [512, 1536], P('rep')
- grad_proj: float32 [512, 512], P('rep')
- grad_conv: float32 [2, 3, 3, 512], replicated
- grad_scale: float32 [2, 512], replicated
The draws below stay inside these ranges and needn't reach their ends.
All inputs are finite; a program needn't handle non-finite values.
Results may differ from the reference program's by a relative error of at most 0.0095.
Values may be sent and summed in bfloat16 or wider, within the bound.
No kernel may reach another device: no remote copies, remote signals or barrier semaphores. Data moves between devices by JAX's collectives and lax.ppermute only.
A program may use at most 64 MiB of HBM per device.

```python
import jax
import jax.numpy as jnp
from jax import lax

D = 512
HEADS = 8
HEAD_DIM = 64
WIDTH = 256
HEIGHT = 16
IMAGES = 4


def draw_incoming_embeddings(key, part):
    shape = (IMAGES, HEIGHT, WIDTH, D)
    lean = jax.random.normal(jax.random.fold_in(key, 2), (IMAGES, 1, 1, D), jnp.float32)
    position = jnp.arange(HEIGHT, dtype=jnp.float32) / max(HEIGHT - 1, 1)
    noise = jax.random.normal(jax.random.fold_in(key, 1), shape, jnp.float32)
    rise = 3.0 * position
    values = noise + rise[None, :, None, None] * lean
    return jnp.clip(values, -16.0, 16.0).astype(jnp.bfloat16)


def draw_triple_mapping_matrix(key, part):
    base = jax.random.normal(key, (D, 3 * D), jnp.float32) * D ** (-0.5)
    return jnp.clip(base, -1.0, 1.0).astype(jnp.bfloat16)


def draw_head_sharpness(key, part):
    uniform_draw = jax.random.uniform(key, (HEADS,), jnp.float32)
    temps = 0.5 * jnp.exp(uniform_draw * jnp.log(8.0))
    return temps


def levels(key, dims, shards, least, high):
    gain, own = 1.0, jax.random.fold_in(key, 6)
    for axis_at, blocks in shards:
        heights = jnp.exp(jax.random.uniform(jax.random.fold_in(own, axis_at), (blocks,), jnp.float32, least / len(shards), high / len(shards)))
        gain = gain * jnp.repeat(heights, dims[axis_at] // blocks).reshape([-1 if axis == axis_at else 1 for axis in range(len(dims))])
    return gain


def bell_draw(rng, extent, scale, bound, shards=(), kind=jnp.bfloat16):
    array = scale * jax.random.normal(rng, extent, jnp.float32)
    if shards:
        array = array * levels(rng, extent, shards, -0.22, 0.18)
    return jnp.clip(array, -bound, bound).astype(kind)


def setup_inputs(seed: int = 0) -> dict:
    key_list = jax.random.split(jax.random.key(seed), 10)
    return {
        "incoming_embeddings": draw_incoming_embeddings(jax.random.fold_in(key_list[9], 71), 0),
        "output_sensitivity": bell_draw(key_list[1], (IMAGES, HEIGHT, WIDTH, D), 1.0, 6.0, ((0, 4), (1, 8))),
        "mixing_prenormal_multiplier": jnp.clip(1.0 + 0.1 * jax.random.normal(key_list[2], (D,), jnp.float32), 0.5, 1.5),
        "triple_mapping_matrix": draw_triple_mapping_matrix(jax.random.fold_in(key_list[9], 71), 0),
        "head_sharpness": draw_head_sharpness(jax.random.fold_in(key_list[9], 71), 0),
        "output_mapping_matrix": bell_draw(key_list[5], (D, D), D ** -0.5, 0.25),
        "residual_arm_factors": jnp.clip(1.0 + 0.1 * jax.random.normal(key_list[6], (2, D), jnp.float32), 0.5, 1.5),
        "locality_prenormal_multiplier": jnp.clip(1.0 + 0.1 * jax.random.normal(key_list[7], (D,), jnp.float32), 0.5, 1.5),
        "separable_kernel_pair": bell_draw(key_list[8], (2, 3, 3, D), 9 ** -0.5, 2.0, (), jnp.float32),
    }


EPS = 1e-06

def conv_valid(padded, kernel):
    row_count = padded.shape[0] - 2
    col_count = padded.shape[1] - 2
    total = jnp.zeros((row_count, col_count, padded.shape[2]), jnp.float32)
    for offset_row in range(3):
        for offset_col in range(3):
            total = total + padded[offset_row:offset_row + row_count, offset_col:offset_col + col_count] * kernel[offset_row, offset_col]
    return total

def gelu_grad(values):
    cumul = 0.5 * (1.0 + lax.erf(values * 0.7071067811865476))
    density = jnp.exp(-0.5 * values * values) * 0.3989422804014327
    return cumul + values * density

def norm_rows(values, gain_vec):
    floated = values.astype(jnp.float32)
    centre = lax.optimization_barrier(jnp.mean(floated, -1, keepdims=True))
    centred = floated - centre
    variance = lax.optimization_barrier(jnp.mean(centred * centred, -1, keepdims=True))
    inverse = lax.rsqrt(variance + EPS)
    normed = centred * inverse
    return (normed * gain_vec, normed, inverse)

def norm_back(upstream, gain_vec, normed, inverse):
    scaled = upstream * gain_vec
    return inverse * (scaled - lax.optimization_barrier(jnp.mean(scaled, -1, keepdims=True)) - normed * lax.optimization_barrier(jnp.mean(scaled * normed, -1, keepdims=True)))

def single_slide_evaluate(slide_embeddings, slide_sensitivities, mixing_prenormal_multiplier, triple_mapping_matrix, head_sharpness, output_mapping_matrix, residual_arm_factors, locality_prenormal_multiplier, separable_kernel_pair):
    high = lax.Precision.HIGHEST
    token_count = HEIGHT * WIDTH
    flat_rows = slide_embeddings.reshape(token_count, D)
    act_one, normed_one, inverse_one = norm_rows(flat_rows, mixing_prenormal_multiplier)
    act_one = act_one.astype(jnp.bfloat16)
    mixed_rows = jnp.dot(act_one, triple_mapping_matrix, preferred_element_type=jnp.float32).astype(jnp.bfloat16)
    query_f = mixed_rows[:, :D].astype(jnp.float32).reshape(token_count, HEADS, HEAD_DIM)
    key_f = mixed_rows[:, D:2 * D].astype(jnp.float32).reshape(token_count, HEADS, HEAD_DIM)
    value_f = mixed_rows[:, 2 * D:].astype(jnp.float32).reshape(token_count, HEADS, HEAD_DIM)
    covariance_accumulated = jnp.einsum('mhc,mhe->hce', query_f, key_f, precision=high)
    query_norm = jnp.sqrt(lax.optimization_barrier(jnp.sum(query_f * query_f, 0)) + EPS)
    key_norm = jnp.sqrt(lax.optimization_barrier(jnp.sum(key_f * key_f, 0)) + EPS)
    softmax_divisor = query_norm[:, :, None] * key_norm[:, None, :]
    feature_affinity_logits = head_sharpness[:, None, None] * covariance_accumulated / softmax_divisor
    shifted = feature_affinity_logits - lax.optimization_barrier(jnp.max(feature_affinity_logits, -1, keepdims=True))
    exponent = jnp.exp(shifted)
    attn_prob = exponent / lax.optimization_barrier(jnp.sum(exponent, -1, keepdims=True))
    prob_low = attn_prob.astype(jnp.bfloat16)
    attended = jnp.einsum('hce,mhe->mhc', prob_low.astype(jnp.float32), value_f, precision=high)
    attended = attended.reshape(token_count, D).astype(jnp.bfloat16)
    projected = jnp.dot(attended, output_mapping_matrix, preferred_element_type=jnp.float32)
    residual = (flat_rows.astype(jnp.float32) + residual_arm_factors[0] * projected).astype(jnp.bfloat16)
    act_two, normed_two, inverse_two = norm_rows(residual, locality_prenormal_multiplier)
    act_two = act_two.astype(jnp.bfloat16)
    upstream = slide_sensitivities.astype(jnp.float32)
    padded_in = jnp.pad(act_two.reshape(HEIGHT, WIDTH, D).astype(jnp.float32), ((1, 1), (1, 1), (0, 0)))
    h_one, back_one = jax.vjp(conv_valid, padded_in, separable_kernel_pair[0])
    hidden = jax.nn.gelu(h_one, approximate=False).astype(jnp.bfloat16)
    padded_hid = jnp.pad(hidden.astype(jnp.float32), ((1, 1), (1, 1), (0, 0)))
    spatial, back_two = jax.vjp(conv_valid, padded_hid, separable_kernel_pair[1])
    d_pad_hid, grad_w_two = back_two(residual_arm_factors[1] * upstream)
    d_h_one = d_pad_hid[1:-1, 1:-1] * gelu_grad(h_one)
    d_pad_in, grad_w_one = back_one(d_h_one)
    d_act_two = d_pad_in[1:-1, 1:-1].reshape(token_count, D)
    up_flat = upstream.reshape(token_count, D)
    scale_two = lax.optimization_barrier(jnp.sum(spatial.reshape(token_count, D) * up_flat, 0))
    d_residual = up_flat + norm_back(d_act_two, locality_prenormal_multiplier, normed_two, inverse_two)
    scale_one = lax.optimization_barrier(jnp.sum(projected * d_residual, 0))
    d_proj = (residual_arm_factors[0] * d_residual).astype(jnp.bfloat16)
    grad_proj = jnp.dot(attended.T, d_proj, preferred_element_type=jnp.float32)
    d_attended = jnp.dot(d_proj, output_mapping_matrix.T, preferred_element_type=jnp.float32).astype(jnp.bfloat16)
    d_att_f = d_attended.astype(jnp.float32).reshape(token_count, HEADS, HEAD_DIM)
    prob_grad = jnp.einsum('mhc,mhe->hce', d_att_f, value_f, precision=high)
    d_value = jnp.einsum('hce,mhc->mhe', prob_low.astype(jnp.float32), d_att_f, precision=high)
    logit_sensitivity = attn_prob * (prob_grad - lax.optimization_barrier(jnp.sum(attn_prob * prob_grad, -1, keepdims=True)))
    covariance_sensitivity = (logit_sensitivity * head_sharpness[:, None, None] / softmax_divisor).astype(jnp.bfloat16).astype(jnp.float32)
    weighted = logit_sensitivity * feature_affinity_logits
    d_qsq = -lax.optimization_barrier(jnp.sum(weighted, -1)) / (2.0 * query_norm * query_norm)
    d_ksq = -lax.optimization_barrier(jnp.sum(weighted, 1)) / (2.0 * key_norm * key_norm)
    d_query = jnp.einsum('hce,mhe->mhc', covariance_sensitivity, key_f, precision=high) + 2.0 * d_qsq * query_f
    d_key = jnp.einsum('hce,mhc->mhe', covariance_sensitivity, query_f, precision=high) + 2.0 * d_ksq * key_f
    d_mixed = jnp.concatenate([d_query.reshape(token_count, D), d_key.reshape(token_count, D), d_value.reshape(token_count, D)], -1).astype(jnp.bfloat16)
    grad_qkv = jnp.dot(act_one.T, d_mixed, preferred_element_type=jnp.float32)
    d_act_one = jnp.dot(d_mixed, triple_mapping_matrix.T, preferred_element_type=jnp.float32)
    d_tokens = (d_residual + norm_back(d_act_one, mixing_prenormal_multiplier, normed_one, inverse_one)).astype(jnp.bfloat16)
    return (d_tokens.reshape(HEIGHT, WIDTH, D), grad_qkv, grad_proj, jnp.stack([grad_w_one, grad_w_two]), jnp.stack([scale_one, scale_two]))

def reference(incoming_embeddings, output_sensitivity, mixing_prenormal_multiplier, triple_mapping_matrix, head_sharpness, output_mapping_matrix, residual_arm_factors, locality_prenormal_multiplier, separable_kernel_pair):

    def one_image(zipped_entries):
        return single_slide_evaluate(zipped_entries[0], zipped_entries[1], mixing_prenormal_multiplier, triple_mapping_matrix, head_sharpness, output_mapping_matrix, residual_arm_factors, locality_prenormal_multiplier, separable_kernel_pair)
    results = lax.map(one_image, (incoming_embeddings, output_sensitivity))
    return (results[0], lax.optimization_barrier(jnp.sum(results[1], 0)), lax.optimization_barrier(jnp.sum(results[2], 0)), lax.optimization_barrier(jnp.sum(results[3], 0)), lax.optimization_barrier(jnp.sum(results[4], 0)))
```

```python
import jax
import jax.numpy as jnp
from jax import lax
from jax.sharding import PartitionSpec as P

EPS = 1e-06
F32 = jnp.float32
BF16 = jnp.bfloat16


def swap_bit(value, axis, bit):
    count = lax.axis_size(axis)
    return lax.ppermute(value, axis, [(i, i ^ bit) for i in range(count)])


def bits_of(axis):
    count = lax.axis_size(axis)
    bits = []
    bit = 1
    while bit < count:
        bits.append(bit)
        bit *= 2
    return bits


def all_sum(value, axis):
    for bit in bits_of(axis):
        value = value + swap_bit(value, axis, bit)
    return value


def own_bit(axis, bit):
    return (lax.axis_index(axis) // bit) % 2


def halve(value, axis, bit, dim):
    mine = own_bit(axis, bit)
    keep = lax.dynamic_index_in_dim(value, mine, dim, False)
    give = lax.dynamic_index_in_dim(value, 1 - mine, dim, False)
    got = swap_bit(give, axis, bit)
    return (keep.astype(F32) + got.astype(F32)).astype(BF16)


def reduce_rows(part):
    rows, cols = part.shape
    rep_bits = bits_of("rep")
    value = part.astype(BF16).reshape((2,) * len(rep_bits) + (-1, cols))
    for bit in rep_bits:
        depth = value.ndim - 3
        value = halve(value, "rep", bit, depth)
    for bit in bits_of("sp"):
        value = halve(value.reshape(2, -1, cols), "sp", bit, 0)
    for bit in reversed(bits_of("sp")):
        other = swap_bit(value, "sp", bit)
        mine = own_bit("sp", bit)
        value = jnp.where(
            mine == 0, jnp.concatenate([value, other]), jnp.concatenate([other, value])
        )
    return value.astype(F32)


def neighbours(value):
    count = lax.axis_size("sp")
    beside = swap_bit(value, "sp", 1)
    hops = [(i, i - 2) for i in range(count) if i % 2 == 1 and i >= 2]
    hops += [(i, i + 2) for i in range(count) if i % 2 == 0 and i + 2 < count]
    beyond = lax.ppermute(beside, "sp", hops)
    even = lax.axis_index("sp") % 2 == 0
    return jnp.where(even, beyond, beside), jnp.where(even, beside, beyond)


def norm_stats(values):
    centred = values - jnp.mean(values, -1, keepdims=True)
    inverse = lax.rsqrt(jnp.mean(centred * centred, -1, keepdims=True) + EPS)
    return centred * inverse, inverse


def norm_back(upstream, gain_vec, normed, inverse):
    scaled = upstream * gain_vec
    return inverse * (
        scaled
        - jnp.mean(scaled, -1, keepdims=True)
        - normed * jnp.mean(scaled * normed, -1, keepdims=True)
    )


def heads_of(rows, heads):
    return rows.reshape(rows.shape[0], heads, -1)


def shift_cols(field, step):
    if step == 0:
        return field
    zeros = jnp.zeros_like(field[:, :1])
    if step > 0:
        return jnp.concatenate([field[:, 1:], zeros], 1)
    return jnp.concatenate([zeros, field[:, :-1]], 1)


def dot32(a, b, dims):
    return lax.dot_general(a, b, (dims, ((), ())), preferred_element_type=F32)


def shards(x4, up4, gain_one, w_qkv, sharp, w_out, factors, gain_two, kernels):
    row_count, width, dim = x4.shape[1:]
    heads = sharp.shape[0]
    tokens = row_count * width
    x_own, up_own = x4[0], up4[0]
    x_above, x_below = neighbours(x_own)
    up_above, up_below = neighbours(up_own)

    flat = x_own.reshape(tokens, dim).astype(F32)
    normed_one, inverse_one = norm_stats(flat)
    act_one = (normed_one * gain_one).astype(BF16)
    mixed = dot32(act_one, w_qkv, ((1,), (0,))).astype(BF16)
    query, key, value = (mixed[:, i * dim : (i + 1) * dim] for i in range(3))
    query_f, key_f = query.astype(F32), key.astype(F32)
    gram = jnp.einsum(
        "mhc,mhe->che", heads_of(query, heads), heads_of(key, heads), preferred_element_type=F32
    ).reshape(-1, dim)
    pack = jnp.concatenate(
        [gram, jnp.sum(query_f * query_f, 0)[None], jnp.sum(key_f * key_f, 0)[None]]
    )
    pack = all_sum(pack, "sp")
    head_dim = dim // heads
    gram = pack[:head_dim].reshape(head_dim, heads, head_dim).transpose(1, 0, 2)
    query_norm = jnp.sqrt(pack[head_dim] + EPS).reshape(heads, head_dim)
    key_norm = jnp.sqrt(pack[head_dim + 1] + EPS).reshape(heads, head_dim)
    divisor = query_norm[:, :, None] * key_norm[:, None, :]
    scores = sharp[:, None, None] * gram / divisor
    prob = jax.nn.softmax(scores, -1)
    prob_low = prob.astype(BF16)

    def token_part(value_rows, flat_rows):
        attended = jnp.einsum(
            "hce,mhe->mhc", prob_low, heads_of(value_rows, heads), preferred_element_type=F32
        ).reshape(-1, dim).astype(BF16)
        projected = dot32(attended, w_out, ((1,), (0,)))
        residual = (flat_rows + factors[0] * projected).astype(BF16).astype(F32)
        normed, inverse = norm_stats(residual)
        act_two = (normed * gain_two).astype(BF16)
        return attended, projected, normed, inverse, act_two

    def edge_part(x_rows):
        flat_rows = x_rows.reshape(-1, dim).astype(F32)
        act = (norm_stats(flat_rows)[0] * gain_one).astype(BF16)
        value_rows = dot32(act, w_qkv[:, 2 * dim :], ((1,), (0,))).astype(BF16)
        return token_part(value_rows, flat_rows)[4].reshape(-1, width, dim)

    attended, projected, normed_two, inverse_two, act_two = token_part(value, flat)
    act_ext = jnp.concatenate(
        [edge_part(x_above[-2:]), act_two.reshape(row_count, width, dim), edge_part(x_below[:2])]
    ).astype(F32)
    up_ext = jnp.concatenate([up_above[-2:], up_own, up_below[:2]]).astype(F32)
    up_two = up_ext * factors[1]
    mid = row_count + 2

    def conv(field, kernel, flip):
        total = 0.0
        for j in range(3):
            column = 0.0
            for i in range(3):
                row = 2 - i if flip else i
                column = column + field[row : row + field.shape[0] - 2] * kernel[i, j]
            total = total + shift_cols(column, 1 - j if flip else j - 1)
        return total

    h_one = conv(act_ext, kernels[0], False)
    d_hidden = conv(up_two, kernels[1], True)
    cumul = 0.5 * (1.0 + lax.erf(h_one * 0.7071067811865476))
    density = jnp.exp(-0.5 * h_one * h_one) * 0.3989422804014327
    d_h = d_hidden * (cumul + h_one * density)
    index = lax.axis_index("sp")
    keep_top = (index > 0).astype(F32)
    keep_bottom = (index < lax.axis_size("sp") - 1).astype(F32)
    keep = jnp.concatenate([keep_top[None], jnp.ones((row_count,), F32), keep_bottom[None]])
    d_h = jnp.where(keep[:, None, None] > 0, d_h, 0.0)
    hidden = (h_one * cumul)[1:-1].astype(BF16).astype(F32)
    d_act = conv(d_h, kernels[0], True).reshape(tokens, dim)
    d_h_own = d_h[1:-1]
    conv_one, conv_two = [], []
    for i in range(3):
        for j in range(3):
            conv_one.append(
                jnp.sum(shift_cols(d_h_own, 1 - j) * act_ext[1 + i : 1 + i + row_count], (0, 1))
            )
            conv_two.append(
                jnp.sum(shift_cols(hidden, j - 1) * up_ext[3 - i : 3 - i + row_count], (0, 1))
            )
    conv_one = jnp.stack(conv_one)
    conv_raw = jnp.stack(conv_two)
    scale_two = jnp.sum(kernels[1].reshape(9, dim) * conv_raw, 0)
    d_res = up_own.reshape(tokens, dim).astype(F32) + norm_back(
        d_act, gain_two, normed_two, inverse_two
    )
    scale_one = jnp.sum(projected * d_res, 0)
    d_proj = (factors[0] * d_res).astype(BF16)
    grad_proj = dot32(attended, d_proj, ((0,), (0,)))
    d_att = dot32(d_proj, w_out, ((1,), (1,))).astype(BF16)
    prob_part = jnp.einsum(
        "mhc,mhe->che", heads_of(d_att, heads), heads_of(value, heads), preferred_element_type=F32
    ).reshape(-1, dim)
    d_value = jnp.einsum(
        "hce,mhc->mhe", prob_low, heads_of(d_att, heads), preferred_element_type=F32
    ).reshape(tokens, dim).astype(BF16)
    grad_v = dot32(act_one, d_value, ((0,), (0,)))
    small = jnp.concatenate(
        [conv_one, conv_raw * factors[1], scale_one[None], scale_two[None]]
    )
    pack = all_sum(jnp.concatenate([prob_part, small]), "sp")
    early = reduce_rows(jnp.concatenate([grad_v, grad_proj], 1))
    small = all_sum(pack[head_dim:], "rep")
    prob_grad = pack[:head_dim].reshape(head_dim, heads, head_dim).transpose(1, 0, 2)
    d_scores = prob * (prob_grad - jnp.sum(prob * prob_grad, -1, keepdims=True))
    d_gram = (d_scores * sharp[:, None, None] / divisor).astype(BF16)
    weighted = d_scores * scores
    d_qsq = -jnp.sum(weighted, -1) / (2.0 * query_norm * query_norm)
    d_ksq = -jnp.sum(weighted, 1) / (2.0 * key_norm * key_norm)
    d_query = (
        jnp.einsum("hce,mhe->mhc", d_gram, heads_of(key, heads), preferred_element_type=F32)
        .reshape(tokens, dim) + 2.0 * d_qsq.reshape(dim) * query_f
    )
    d_key = (
        jnp.einsum("hce,mhc->mhe", d_gram, heads_of(query, heads), preferred_element_type=F32)
        .reshape(tokens, dim) + 2.0 * d_ksq.reshape(dim) * key_f
    )
    d_qk = jnp.concatenate([d_query, d_key], -1).astype(BF16)
    late = reduce_rows(dot32(act_one, d_qk, ((0,), (0,))))
    d_act_one = dot32(d_qk, w_qkv[:, : 2 * dim], ((1,), (1,))) + dot32(
        d_value, w_qkv[:, 2 * dim :], ((1,), (1,))
    )
    grad_input = (d_res + norm_back(d_act_one, gain_one, normed_one, inverse_one)).astype(BF16)
    return (
        grad_input.reshape(1, row_count, width, dim),
        jnp.concatenate([late, early[:, :dim]], 1),
        early[:, dim:],
        small[:18].reshape(2, 3, 3, dim),
        small[18:20],
    )


def solution(mesh):
    rows = P("rep", "sp", None, None)
    return jax.shard_map(
        shards,
        mesh=mesh,
        in_specs=(rows, rows) + (P(),) * 7,
        out_specs=(rows, P("rep", None), P("rep", None), P(), P()),
        check_vma=False,
    )
```

```python
import functools

import jax
import jax.numpy as jnp
from jax import lax
from jax.experimental import pallas as pl
from jax.experimental.pallas import tpu as pltpu
from jax.sharding import PartitionSpec as P

EPS = 1e-06
F32 = jnp.float32
BF16 = jnp.bfloat16
LANES = 128
PAD = 8
COLS = 64
EDGE = 2


def swap_bit(value, axis, bit):
    count = lax.axis_size(axis)
    return lax.ppermute(value, axis, [(i, i ^ bit) for i in range(count)])


def bits_of(axis):
    count = lax.axis_size(axis)
    bits = []
    bit = 1
    while bit < count:
        bits.append(bit)
        bit *= 2
    return bits


def all_sum(value, axis):
    for bit in bits_of(axis):
        value = value + swap_bit(value, axis, bit)
    return value


def own_bit(axis, bit):
    return (lax.axis_index(axis) // bit) % 2


def halve(value, axis, bit, dim):
    mine = own_bit(axis, bit)
    keep = lax.dynamic_index_in_dim(value, mine, dim, False)
    give = lax.dynamic_index_in_dim(value, 1 - mine, dim, False)
    got = swap_bit(give, axis, bit)
    return (keep.astype(F32) + got.astype(F32)).astype(BF16)


def reduce_rows(part):
    rows, cols = part.shape
    rep_bits = bits_of("rep")
    value = part.reshape((2,) * len(rep_bits) + (-1, cols))
    for bit in rep_bits:
        depth = value.ndim - 3
        value = halve(value, "rep", bit, depth)
    for bit in bits_of("sp"):
        value = halve(value.reshape(2, -1, cols), "sp", bit, 0)
    for bit in reversed(bits_of("sp")):
        other = swap_bit(value, "sp", bit)
        mine = own_bit("sp", bit)
        value = jnp.where(
            mine == 0, jnp.concatenate([value, other]), jnp.concatenate([other, value])
        )
    return value.astype(F32)


def dot32(a, b, left, right):
    return lax.dot_general(a, b, (((left,), (right,)), ((), ())), preferred_element_type=F32)


def norm_stats(values):
    centred = values - jnp.mean(values, -1, keepdims=True)
    inverse = lax.rsqrt(jnp.mean(centred * centred, -1, keepdims=True) + EPS)
    return centred * inverse, inverse


def norm_back(upstream, gain_vec, normed, inverse):
    scaled = upstream * gain_vec
    return inverse * (
        scaled
        - jnp.mean(scaled, -1, keepdims=True)
        - normed * jnp.mean(scaled * normed, -1, keepdims=True)
    )


def masks(head_dim):
    lane = lax.broadcasted_iota(jnp.int32, (head_dim, LANES), 1)
    row = lax.broadcasted_iota(jnp.int32, (head_dim, LANES), 0)
    return lane // head_dim, lane % head_dim == row


def by_head(block_id, parts):
    out = parts[-1]
    for index in range(len(parts) - 2, -1, -1):
        out = jnp.where(block_id == index, parts[index], out)
    return out


def seg_reduce(block_id, value, fill, func):
    count = LANES // value.shape[0]
    parts = [
        func(jnp.where(block_id == index, value, fill), -1, keepdims=True) for index in range(count)
    ]
    return by_head(block_id, parts)


def seg_sum(block_id, value):
    return seg_reduce(block_id, value, 0.0, jnp.sum)


def block_diag(block_id, value):
    count = LANES // value.shape[0]
    return jnp.concatenate(
        [jnp.where(block_id == index, value, 0.0) for index in range(count)], 0
    ).astype(BF16)


def compact(block_id, full):
    head_dim = block_id.shape[0]
    count = LANES // head_dim
    return by_head(block_id, [full[i * head_dim : (i + 1) * head_dim] for i in range(count)])


def softmax_block(pack_ref, sharp_ref, block, head_dim):
    block_id, diag = masks(head_dim)
    lanes = slice(block * LANES, (block + 1) * LANES)
    count = LANES // head_dim
    gram = pack_ref[:head_dim, lanes]
    query_row = jnp.sqrt(pack_ref[head_dim : head_dim + 1, lanes] + EPS)
    key_row = jnp.sqrt(pack_ref[head_dim + 1 : head_dim + 2, lanes] + EPS)
    query_col = seg_sum(block_id, jnp.where(diag, query_row, 0.0))
    sharp = by_head(block_id, [sharp_ref[block * count + i] for i in range(count)])
    divisor = query_col * key_row
    scores = sharp * gram / divisor
    shifted = scores - seg_reduce(block_id, scores, -jnp.inf, jnp.max)
    exponent = jnp.exp(shifted)
    prob = exponent / seg_sum(block_id, exponent)
    return prob, scores, sharp, divisor, query_col, key_row, block_id, diag


def first_kernel(x_ref, gain_ref, w_ref, mixed_ref, act_ref, pack_ref, *, head_dim):
    tokens, dim = x_ref.shape
    step = 64

    @pl.loop(0, tokens // step)
    def _(index):
        rows = pl.ds(pl.multiple_of(index * step, step), step)
        normed, _ = norm_stats(x_ref[rows, :].astype(F32))
        act_ref[rows, :] = (normed * gain_ref[...]).astype(BF16)

    act = act_ref[...]
    for part in range(w_ref.shape[1] // 256):
        cols = slice(part * 256, part * 256 + 256)
        mixed_ref[:, cols] = dot32(act, w_ref[:, cols], 1, 0).astype(BF16)
    block_id, _ = masks(head_dim)
    pack_ref[head_dim:, :] = jnp.zeros_like(pack_ref[head_dim:, :])
    for block in range(dim // LANES):
        lanes = slice(block * LANES, (block + 1) * LANES)
        query = mixed_ref[:, lanes]
        key = mixed_ref[:, dim + block * LANES : dim + (block + 1) * LANES]
        pack_ref[:head_dim, lanes] = compact(block_id, dot32(query, key, 0, 0))
        for row, value in enumerate((query, key)):
            value = value.astype(F32)
            pack_ref[head_dim + row : head_dim + row + 1, lanes] = jnp.sum(
                value * value, 0, keepdims=True
            )


def shift_sum(parts):
    size = parts[1].shape[0]
    return pltpu.roll(parts[0], 1, 0) + parts[1] + pltpu.roll(parts[2], size - 1, 0)


def inner(value):
    return value[PAD:-PAD]


def row_taps(ref, rows, window, lanes, kernel, flip):
    loaded = [ref[row, window, lanes] for row in rows]
    parts = []
    for j in range(3):
        total = None
        for i in range(3):
            tap = kernel[3 * i + j]
            term = loaded[2 - i if flip else i] * tap
            total = term if total is None else total + term
        parts.append(total)
    return shift_sum(parts[::-1] if flip else parts)


def for_tiles(width, dim, body):
    @pl.loop(0, dim // LANES)
    def _(block):
        lanes = pl.ds(pl.multiple_of(block * LANES, LANES), LANES)

        @pl.loop(0, width // COLS)
        def _(part):
            start = pl.multiple_of(part * COLS, COLS)
            body(start, lanes)


def attend_kernel(
    edge_ref, sharp_ref, pack_ref, x_ref, near_ref, far_ref, value_ref, gain_one_ref, gain_two_ref,
    factor_ref, w_value_ref, w_out_ref, kernel_ref,
    attended_ref, projected_ref, residual_ref, act_mid_ref, hidden_ref, slope_ref, act_ext, diag_ref,
):
    rows, width, dim = x_ref.shape
    head_dim = dim // sharp_ref.shape[0]
    blocks = dim // LANES
    for block in range(blocks):
        prob, *_, block_id, _ = softmax_block(pack_ref, sharp_ref, block, head_dim)
        diag_ref[block] = block_diag(block_id, prob)
    act_ext[:, :PAD] = jnp.zeros_like(act_ext[:, :PAD])
    act_ext[:, PAD + width :] = jnp.zeros_like(act_ext[:, PAD + width :])

    def token_part(x_rows, value, place, own):
        parts = []
        for block in range(blocks):
            lanes = slice(block * LANES, (block + 1) * LANES)
            parts.append(dot32(value[:, lanes], diag_ref[block], 1, 1).astype(BF16))
        attended = jnp.concatenate(parts, 1)
        projected = dot32(attended, w_out_ref[...], 1, 0)
        residual = (x_rows + factor_ref[0:1, :] * projected).astype(BF16)
        normed, _ = norm_stats(residual.astype(F32))
        act = (normed * gain_two_ref[...]).astype(BF16)
        act_ext[place, PAD : PAD + width, :] = act.astype(F32)
        if own is not None:
            span = slice(own * width, (own + 1) * width)
            attended_ref[span, :] = attended
            projected_ref[span, :] = projected
            residual_ref[span, :] = residual

    for row in range(rows):
        value = value_ref[row * width : (row + 1) * width, :]
        token_part(x_ref[row].astype(F32), value, EDGE + row, row)
    even = edge_ref[0]
    for ref, place, source in (
        (near_ref, even * (rows + EDGE), (1 - even) * (rows - EDGE)),
        (far_ref, (1 - even) * (rows + EDGE), even * (rows - EDGE)),
    ):
        for row in range(EDGE):
            x_rows = ref[source + row].astype(F32)
            normed, _ = norm_stats(x_rows)
            act = (normed * gain_one_ref[...]).astype(BF16)
            value = dot32(act, w_value_ref[...], 1, 0).astype(BF16)
            token_part(x_rows, value, place + row, None)
    for row in range(rows + 2):
        act_mid_ref[row] = act_ext[row + 1, PAD : PAD + width, :].astype(BF16)

    def tile(start, lanes):
        window = pl.ds(start, COLS + 2 * PAD)
        cols = pl.ds(start, COLS)
        kernel = [kernel_ref[tap : tap + 1, lanes] for tap in range(9)]
        for row in range(rows + 2):
            h_one = inner(row_taps(act_ext, (row, row + 1, row + 2), window, lanes, kernel, False))
            cumul = 0.5 * (1.0 + lax.erf(h_one * 0.7071067811865476))
            density = jnp.exp(-0.5 * h_one * h_one) * 0.3989422804014327
            slope_ref[row, cols, lanes] = cumul + h_one * density
            if 1 <= row <= rows:
                hidden_ref[row - 1, cols, lanes] = (h_one * cumul).astype(BF16)

    for_tiles(width, dim, tile)


def back_kernel(
    edge_ref, sharp_ref, pack_ref, up_ref, near_ref, far_ref, act_mid_ref, hidden_ref, slope_ref,
    attended_ref, projected_ref, residual_ref, value_ref, act_one_ref, gain_two_ref, factor_ref,
    w_out_ref, kernel_ref,
    pack_out_ref, d_res_ref, d_value_ref, grad_ref,
    up_ext, d_ext, hid_ext, d_act, sums, d_proj_ref, d_att_ref,
):
    rows, width, dim = up_ref.shape
    head_dim = dim // sharp_ref.shape[0]
    blocks = dim // LANES
    for ref in (up_ext, d_ext, hid_ext):
        ref[:, :PAD] = jnp.zeros_like(ref[:, :PAD])
        ref[:, PAD + width :] = jnp.zeros_like(ref[:, PAD + width :])
    sums[...] = jnp.zeros_like(sums)
    main = slice(PAD, PAD + width)
    even = edge_ref[0]
    for row in range(rows):
        up_ext[EDGE + row, main, :] = up_ref[row].astype(F32)
        hid_ext[row, main, :] = hidden_ref[row].astype(F32)
    for ref, place, source in (
        (near_ref, even * (rows + EDGE), (1 - even) * (rows - EDGE)),
        (far_ref, (1 - even) * (rows + EDGE), even * (rows - EDGE)),
    ):
        for row in range(EDGE):
            up_ext[place + row, main, :] = ref[source + row].astype(F32)

    def d_hidden_tile(start, lanes):
        window = pl.ds(start, COLS + 2 * PAD)
        cols = pl.ds(start, COLS)
        factor = factor_ref[1:2, lanes]
        kernel = [kernel_ref[9 + tap : 10 + tap, lanes] * factor for tap in range(9)]
        for row in range(rows + 2):
            d_hidden = inner(row_taps(up_ext, (row, row + 1, row + 2), window, lanes, kernel, True))
            d_h = d_hidden * slope_ref[row, cols, lanes]
            if row == 0:
                d_h = jnp.where(edge_ref[1] > 0, d_h, 0.0)
            if row == rows + 1:
                d_h = jnp.where(edge_ref[2] > 0, d_h, 0.0)
            d_ext[row, pl.ds(start + PAD, COLS), lanes] = d_h

    for_tiles(width, dim, d_hidden_tile)

    def fold(value):
        return jnp.sum(value.reshape(-1, 8, LANES), 0)

    def d_act_tile(start, lanes):
        window = pl.ds(start, COLS + 2 * PAD)
        cols = pl.ds(start, COLS)
        kernel = [kernel_ref[tap : tap + 1, lanes] for tap in range(9)]
        size = COLS + 2 * PAD
        shifts = (1, 0, size - 1)
        for row in range(rows):
            d_act[row, cols, lanes] = inner(
                row_taps(d_ext, (row, row + 1, row + 2), window, lanes, kernel, True)
            )
        act = [act_mid_ref[row, cols, lanes].astype(F32) for row in range(rows + 2)]
        moved = [
            [inner(pltpu.roll(d_ext[1 + row, window, lanes], shifts[2 - j], 0)) if j != 1
             else inner(d_ext[1 + row, window, lanes]) for j in range(3)]
            for row in range(rows)
        ]
        for i in range(3):
            for j in range(3):
                total = moved[0][j] * act[i]
                for row in range(1, rows):
                    total = total + moved[row][j] * act[i + row]
                sums[3 * i + j, :, lanes] += fold(total)
        up = [up_ext[1 + row, pl.ds(start + PAD, COLS), lanes] for row in range(rows + 2)]
        moved = [
            [inner(pltpu.roll(hid_ext[row, window, lanes], shifts[j], 0)) if j != 1
             else inner(hid_ext[row, window, lanes]) for j in range(3)]
            for row in range(rows)
        ]
        for i in range(3):
            for j in range(3):
                total = moved[0][j] * up[2 - i]
                for row in range(1, rows):
                    total = total + moved[row][j] * up[2 - i + row]
                sums[9 + 3 * i + j, :, lanes] += fold(total)

    for_tiles(width, dim, d_act_tile)

    factor_one, factor_two = factor_ref[0:1, :], factor_ref[1:2, :]
    scale_one = jnp.zeros((1, dim), F32)
    step = 64
    for row in range(rows):
        for part in range(width // step):
            span = slice(row * width + part * step, row * width + (part + 1) * step)
            cols = slice(part * step, (part + 1) * step)
            normed, inverse = norm_stats(residual_ref[span, :].astype(F32))
            d_res = up_ref[row, cols, :].astype(F32) + norm_back(
                d_act[row, cols, :], gain_two_ref[...], normed, inverse
            )
            d_res_ref[span, :] = d_res
            scale_one = scale_one + jnp.sum(projected_ref[span, :] * d_res, 0, keepdims=True)
            d_proj_ref[span, :] = (factor_one * d_res).astype(BF16)
    scale_two = jnp.zeros((1, dim), F32)
    for tap in range(9):
        pack_out_ref[head_dim + tap : head_dim + tap + 1, :] = jnp.sum(sums[tap], 0, keepdims=True)
        raw = jnp.sum(sums[9 + tap], 0, keepdims=True)
        pack_out_ref[head_dim + 9 + tap : head_dim + 10 + tap, :] = raw * factor_two
        scale_two = scale_two + raw * kernel_ref[9 + tap : 10 + tap, :]
    pack_out_ref[head_dim + 18 : head_dim + 19, :] = scale_one
    pack_out_ref[head_dim + 19 : head_dim + 20, :] = scale_two
    pack_out_ref[head_dim + 20 :, :] = jnp.zeros_like(pack_out_ref[head_dim + 20 :, :])
    d_att_ref[...] = dot32(d_proj_ref[...], w_out_ref[...], 1, 1).astype(BF16)
    for block in range(blocks):
        lanes = slice(block * LANES, (block + 1) * LANES)
        prob, *_, block_id, _ = softmax_block(pack_ref, sharp_ref, block, head_dim)
        d_att = d_att_ref[:, lanes]
        pack_out_ref[:head_dim, lanes] = compact(block_id, dot32(d_att, value_ref[:, lanes], 0, 0))
        d_value_ref[:, lanes] = dot32(d_att, block_diag(block_id, prob), 1, 0).astype(BF16)
    grad_ref[:, :dim] = dot32(act_one_ref[...], d_value_ref[...], 0, 0).astype(BF16)
    grad_ref[:, dim:] = dot32(attended_ref[...], d_proj_ref[...], 0, 0).astype(BF16)


def gram_kernel(
    sharp_ref, pack_ref, prob_ref, mixed_ref, act_ref, d_qk_ref, grad_ref,
):
    tokens, dim = act_ref.shape
    head_dim = dim // sharp_ref.shape[0]
    for block in range(dim // LANES):
        lanes = slice(block * LANES, (block + 1) * LANES)
        key_lanes = slice(dim + block * LANES, dim + (block + 1) * LANES)
        prob, scores, sharp, divisor, query_col, key_row, block_id, diag = softmax_block(
            pack_ref, sharp_ref, block, head_dim
        )
        prob_grad = prob_ref[:head_dim, lanes]
        d_scores = prob * (prob_grad - seg_sum(block_id, prob * prob_grad))
        d_gram = block_diag(block_id, d_scores * sharp / divisor)
        weighted = d_scores * scores
        d_qsq_col = -seg_sum(block_id, weighted) / (2.0 * query_col * query_col)
        d_qsq = jnp.sum(jnp.where(diag, d_qsq_col, 0.0), 0, keepdims=True)
        d_ksq = -jnp.sum(weighted, 0, keepdims=True) / (2.0 * key_row * key_row)
        query, key = mixed_ref[:, lanes], mixed_ref[:, key_lanes]
        d_query = dot32(key, d_gram, 1, 1) + 2.0 * d_qsq * query.astype(F32)
        d_key = dot32(query, d_gram, 1, 0) + 2.0 * d_ksq * key.astype(F32)
        d_qk_ref[:, lanes] = d_query.astype(BF16)
        d_qk_ref[:, key_lanes] = d_key.astype(BF16)
    act = act_ref[...]
    for part in range(2 * dim // 256):
        cols = slice(part * 256, part * 256 + 256)
        grad_ref[:, cols] = dot32(act, d_qk_ref[:, cols], 0, 0).astype(BF16)


def input_kernel(x_ref, gain_ref, w_ref, d_qk_ref, d_value_ref, d_res_ref, out_ref):
    tokens, dim = x_ref.shape
    step = 128
    for part in range(tokens // step):
        rows = slice(part * step, (part + 1) * step)
        d_act = dot32(d_qk_ref[rows, :], w_ref[:, : 2 * dim], 1, 1) + dot32(
            d_value_ref[rows, :], w_ref[:, 2 * dim :], 1, 1
        )
        normed, inverse = norm_stats(x_ref[rows, :].astype(F32))
        out_ref[rows, :] = (
            d_res_ref[rows, :] + norm_back(d_act, gain_ref[...], normed, inverse)
        ).astype(BF16)


def call(body, name, outs, args, scalars=0, scratch=()):
    specs = [
        pl.BlockSpec(memory_space=pltpu.SMEM if i < scalars else pltpu.VMEM)
        for i in range(len(args))
    ]
    return pl.pallas_call(
        body,
        name=name,
        out_shape=[jax.ShapeDtypeStruct(shape, dtype) for shape, dtype in outs],
        in_specs=specs,
        out_specs=[pl.BlockSpec(memory_space=pltpu.VMEM)] * len(outs),
        scratch_shapes=[pltpu.VMEM(shape, dtype) for shape, dtype in scratch],
    )(*args)


def beside(value):
    return swap_bit(value, "sp", 1)


def beyond(value):
    count = lax.axis_size("sp")
    hops = [(i, i - 2) for i in range(count) if i % 2 == 1 and i >= 2]
    hops += [(i, i + 2) for i in range(count) if i % 2 == 0 and i + 2 < count]
    return lax.ppermute(value, "sp", hops)


def shards(x4, up4, gain_one, w_qkv, sharp, w_out, factors, gain_two, kernels):
    rows, width, dim = x4.shape[1:]
    heads = sharp.shape[0]
    head_dim = dim // heads
    tokens = rows * width
    x_own, up_own = x4[0], up4[0]
    flat = x_own.reshape(tokens, dim)
    gain_one, gain_two = gain_one[None], gain_two[None]
    taps = kernels.reshape(-1, dim)
    index = lax.axis_index("sp")
    last = lax.axis_size("sp") - 1
    edges = jnp.stack([1 - index % 2, (index > 0).astype(jnp.int32), (index < last).astype(jnp.int32)])
    pack_rows = head_dim + 8

    x_near = beside(x_own)
    mixed, act_one, pack = call(
        functools.partial(first_kernel, head_dim=head_dim), "first",
        [((tokens, 3 * dim), BF16), ((tokens, dim), BF16), ((pack_rows, dim), F32)],
        (flat, gain_one, w_qkv),
    )
    x_far = beyond(x_near)
    up_near = beside(up_own)
    up_far = beyond(up_near)
    pack = all_sum(pack, "sp")
    value = mixed[:, 2 * dim :]
    attended, projected, residual, act_mid, hidden, slope = call(
        attend_kernel, "attend",
        [((tokens, dim), BF16), ((tokens, dim), F32), ((tokens, dim), BF16),
         ((rows + 2, width, dim), BF16), ((rows, width, dim), BF16), ((rows + 2, width, dim), F32)],
        (edges, sharp, pack, x_own, x_near, x_far, value, gain_one, gain_two, factors,
         w_qkv[:, 2 * dim :], w_out, taps),
        scalars=2,
        scratch=[((rows + 2 * EDGE, width + 2 * PAD, dim), F32), ((dim // LANES, LANES, LANES), BF16)],
    )
    small_rows = head_dim + 24
    pack_two, d_res, d_value, grad_early = call(
        back_kernel, "back",
        [((small_rows, dim), F32), ((tokens, dim), F32), ((tokens, dim), BF16), ((dim, 2 * dim), BF16)],
        (edges, sharp, pack, up_own, up_near, up_far, act_mid, hidden, slope, attended, projected,
         residual, value, act_one, gain_two, factors, w_out, taps),
        scalars=2,
        scratch=[((rows + 2 * EDGE, width + 2 * PAD, dim), F32),
                 ((rows + 2, width + 2 * PAD, dim), F32), ((rows, width + 2 * PAD, dim), F32),
                 ((rows, width, dim), F32), ((18, 8, dim), F32), ((tokens, dim), BF16),
                 ((tokens, dim), BF16)],
    )
    pack_two = all_sum(pack_two, "sp")
    d_qk, grad_late = call(
        gram_kernel, "gram",
        [((tokens, 2 * dim), BF16), ((dim, 2 * dim), BF16)],
        (sharp, pack, pack_two, mixed, act_one), scalars=1,
    )
    early = reduce_rows(grad_early)
    late = reduce_rows(grad_late)
    small = all_sum(pack_two[head_dim:], "rep")
    (grad_input,) = call(
        input_kernel, "input", [((tokens, dim), BF16)],
        (flat, gain_one, w_qkv, d_qk, d_value, d_res),
    )
    return (
        grad_input.reshape(1, rows, width, dim),
        jnp.concatenate([late, early[:, :dim]], 1),
        early[:, dim:],
        small[:18].reshape(kernels.shape),
        small[18:20],
    )


def solution(mesh):
    rows = P("rep", "sp", None, None)
    return jax.shard_map(
        shards,
        mesh=mesh,
        in_specs=(rows, rows) + (P(),) * 7,
        out_specs=(rows, P("rep", None), P("rep", None), P(), P()),
        check_vma=False,
    )
```

```python
import functools

import jax
import jax.numpy as jnp
from jax import lax
from jax.experimental import pallas as pl
from jax.experimental.pallas import tpu as pltpu
from jax.sharding import PartitionSpec as P

EPS = 1e-06
F32 = jnp.float32
BF16 = jnp.bfloat16
LANES = 128
PAD = 8
COLS = 64
EDGE = 2


def swap_bit(value, axis, bit):
    count = lax.axis_size(axis)
    return lax.ppermute(value, axis, [(i, i ^ bit) for i in range(count)])


def bits_of(axis):
    count = lax.axis_size(axis)
    bits = []
    bit = 1
    while bit < count:
        bits.append(bit)
        bit *= 2
    return bits


def all_sum(value, axis):
    for bit in bits_of(axis):
        value = value + swap_bit(value, axis, bit)
    return value


def own_bit(axis, bit):
    return (lax.axis_index(axis) // bit) % 2


def add_low(parts):
    total = parts[0].astype(F32)
    for part in parts[1:]:
        total = total + part.astype(F32)
    return total.astype(BF16)


def member(axis, bits):
    return sum(own_bit(axis, bit) << place for place, bit in enumerate(bits))


def spread(bits, offset):
    return sum(bit for place, bit in enumerate(bits) if (offset >> place) & 1)


def scatter_stage(value, axis, bits, dim):
    mine = member(axis, bits)
    parts = [lax.dynamic_index_in_dim(value, mine, dim, False)]
    for offset in range(1, 1 << len(bits)):
        give = lax.dynamic_index_in_dim(value, mine ^ offset, dim, False)
        parts.append(swap_bit(give, axis, spread(bits, offset)))
    return add_low(parts)


def gather_stage(value, axis, bits):
    mine = member(axis, bits)
    parts = [value]
    for offset in range(1, 1 << len(bits)):
        parts.append(swap_bit(value, axis, spread(bits, offset)))
    out = []
    for piece in range(len(parts)):
        chosen = parts[0]
        for offset in range(1, len(parts)):
            chosen = jnp.where(mine == piece ^ offset, parts[offset], chosen)
        out.append(chosen)
    return jnp.concatenate(out)


def stages_of(axis):
    bits = bits_of(axis)
    return [bits[:1]] + [bits[i : i + 2] for i in range(1, len(bits), 2)]


def reduce_rows(keep, give):
    cols = keep.shape[-1]
    bits = bits_of("rep")
    value = add_low([keep, swap_bit(give, "rep", bits[0])])
    for bit in bits[1:]:
        value = value.reshape(-1, 2, value.shape[-2], cols)
        value = scatter_stage(value, "rep", [bit], 1)
    value = value.reshape(-1, cols)
    for bits in stages_of("sp"):
        value = scatter_stage(value.reshape(1 << len(bits), -1, cols), "sp", bits, 0)
    for bits in reversed(stages_of("sp")):
        value = gather_stage(value, "sp", bits)
    return value.astype(F32)


def dot32(a, b, left, right):
    return lax.dot_general(a, b, (((left,), (right,)), ((), ())), preferred_element_type=F32)


def norm_stats(values):
    centred = values - jnp.mean(values, -1, keepdims=True)
    inverse = lax.rsqrt(jnp.mean(centred * centred, -1, keepdims=True) + EPS)
    return centred * inverse, inverse


def norm_back(upstream, gain_vec, normed, inverse):
    scaled = upstream * gain_vec
    return inverse * (
        scaled
        - jnp.mean(scaled, -1, keepdims=True)
        - normed * jnp.mean(scaled * normed, -1, keepdims=True)
    )


def masks(head_dim):
    lane = lax.broadcasted_iota(jnp.int32, (head_dim, LANES), 1)
    row = lax.broadcasted_iota(jnp.int32, (head_dim, LANES), 0)
    return lane // head_dim, lane % head_dim == row


def by_head(block_id, parts):
    out = parts[-1]
    for index in range(len(parts) - 2, -1, -1):
        out = jnp.where(block_id == index, parts[index], out)
    return out


def seg_reduce(block_id, value, fill, func):
    count = LANES // value.shape[0]
    parts = [
        func(jnp.where(block_id == index, value, fill), -1, keepdims=True) for index in range(count)
    ]
    return by_head(block_id, parts)


def seg_sum(block_id, value):
    return seg_reduce(block_id, value, 0.0, jnp.sum)


def block_diag(block_id, value):
    count = LANES // value.shape[0]
    return jnp.concatenate(
        [jnp.where(block_id == index, value, 0.0) for index in range(count)], 0
    ).astype(BF16)


def compact(block_id, full):
    head_dim = block_id.shape[0]
    count = LANES // head_dim
    return by_head(block_id, [full[i * head_dim : (i + 1) * head_dim] for i in range(count)])


def softmax_block(pack_ref, sharp_ref, block, head_dim):
    block_id, diag = masks(head_dim)
    lanes = slice(block * LANES, (block + 1) * LANES)
    count = LANES // head_dim
    gram = pack_ref[:head_dim, lanes]
    query_row = jnp.sqrt(pack_ref[head_dim : head_dim + 1, lanes] + EPS)
    key_row = jnp.sqrt(pack_ref[head_dim + 1 : head_dim + 2, lanes] + EPS)
    query_col = seg_sum(block_id, jnp.where(diag, query_row, 0.0))
    sharp = by_head(block_id, [sharp_ref[block * count + i] for i in range(count)])
    divisor = query_col * key_row
    scores = sharp * gram / divisor
    shifted = scores - seg_reduce(block_id, scores, -jnp.inf, jnp.max)
    exponent = jnp.exp(shifted)
    prob = exponent / seg_sum(block_id, exponent)
    return prob, scores, sharp, divisor, query_col, key_row, block_id, diag


def first_kernel(x_ref, gain_ref, w_ref, mixed_ref, act_ref, pack_ref, *, head_dim):
    tokens, dim = x_ref.shape
    step = 64

    @pl.loop(0, tokens // step)
    def _(index):
        rows = pl.ds(pl.multiple_of(index * step, step), step)
        normed, _ = norm_stats(x_ref[rows, :].astype(F32))
        act_ref[rows, :] = (normed * gain_ref[...]).astype(BF16)

    act = act_ref[...]
    for part in range(w_ref.shape[1] // 256):
        cols = slice(part * 256, part * 256 + 256)
        mixed_ref[:, cols] = dot32(act, w_ref[:, cols], 1, 0).astype(BF16)
    block_id, _ = masks(head_dim)
    pack_ref[head_dim:, :] = jnp.zeros_like(pack_ref[head_dim:, :])
    for block in range(dim // LANES):
        lanes = slice(block * LANES, (block + 1) * LANES)
        query = mixed_ref[:, lanes]
        key = mixed_ref[:, dim + block * LANES : dim + (block + 1) * LANES]
        pack_ref[:head_dim, lanes] = compact(block_id, dot32(query, key, 0, 0))
        for row, value in enumerate((query, key)):
            value = value.astype(F32)
            pack_ref[head_dim + row : head_dim + row + 1, lanes] = jnp.sum(
                value * value, 0, keepdims=True
            )


def shift_sum(parts):
    size = parts[1].shape[0]
    return pltpu.roll(parts[0], 1, 0) + parts[1] + pltpu.roll(parts[2], size - 1, 0)


def inner(value):
    return value[PAD:-PAD]


def row_taps(ref, rows, window, lanes, kernel, flip):
    loaded = [ref[row, window, lanes] for row in rows]
    parts = []
    for j in range(3):
        total = None
        for i in range(3):
            tap = kernel[3 * i + j]
            term = loaded[2 - i if flip else i] * tap
            total = term if total is None else total + term
        parts.append(total)
    return shift_sum(parts[::-1] if flip else parts)


def for_tiles(width, dim, body):
    @pl.loop(0, dim // LANES)
    def _(block):
        lanes = pl.ds(pl.multiple_of(block * LANES, LANES), LANES)

        @pl.loop(0, width // COLS)
        def _(part):
            start = pl.multiple_of(part * COLS, COLS)
            body(start, lanes)


def attend_kernel(
    edge_ref, sharp_ref, pack_ref, x_ref, near_ref, far_ref, value_ref, gain_one_ref, gain_two_ref,
    factor_ref, w_value_ref, w_out_ref, kernel_ref,
    attended_ref, projected_ref, residual_ref, act_mid_ref, hidden_ref, slope_ref, act_ext, diag_ref,
):
    rows, width, dim = x_ref.shape
    head_dim = dim // sharp_ref.shape[0]
    blocks = dim // LANES
    for block in range(blocks):
        prob, *_, block_id, _ = softmax_block(pack_ref, sharp_ref, block, head_dim)
        diag_ref[block] = block_diag(block_id, prob)
    act_ext[:, :PAD] = jnp.zeros_like(act_ext[:, :PAD])
    act_ext[:, PAD + width :] = jnp.zeros_like(act_ext[:, PAD + width :])

    def token_part(x_rows, value, place, own):
        parts = []
        for block in range(blocks):
            lanes = slice(block * LANES, (block + 1) * LANES)
            parts.append(dot32(value[:, lanes], diag_ref[block], 1, 1).astype(BF16))
        attended = jnp.concatenate(parts, 1)
        projected = dot32(attended, w_out_ref[...], 1, 0)
        residual = (x_rows + factor_ref[0:1, :] * projected).astype(BF16)
        normed, _ = norm_stats(residual.astype(F32))
        act = (normed * gain_two_ref[...]).astype(BF16)
        act_ext[place, PAD : PAD + width, :] = act.astype(F32)
        if own is not None:
            span = slice(own * width, (own + 1) * width)
            attended_ref[span, :] = attended
            projected_ref[span, :] = projected
            residual_ref[span, :] = residual

    for row in range(rows):
        value = value_ref[row * width : (row + 1) * width, :]
        token_part(x_ref[row].astype(F32), value, EDGE + row, row)
    even = edge_ref[0]
    for ref, place, source in (
        (near_ref, even * (rows + EDGE), (1 - even) * (rows - EDGE)),
        (far_ref, (1 - even) * (rows + EDGE), even * (rows - EDGE)),
    ):
        for row in range(EDGE):
            x_rows = ref[source + row].astype(F32)
            normed, _ = norm_stats(x_rows)
            act = (normed * gain_one_ref[...]).astype(BF16)
            value = dot32(act, w_value_ref[...], 1, 0).astype(BF16)
            token_part(x_rows, value, place + row, None)
    for row in range(rows + 2):
        act_mid_ref[row] = act_ext[row + 1, PAD : PAD + width, :].astype(BF16)

    def tile(start, lanes):
        window = pl.ds(start, COLS + 2 * PAD)
        cols = pl.ds(start, COLS)
        kernel = [kernel_ref[tap : tap + 1, lanes] for tap in range(9)]
        for row in range(rows + 2):
            h_one = inner(row_taps(act_ext, (row, row + 1, row + 2), window, lanes, kernel, False))
            cumul = 0.5 * (1.0 + lax.erf(h_one * 0.7071067811865476))
            density = jnp.exp(-0.5 * h_one * h_one) * 0.3989422804014327
            slope_ref[row, cols, lanes] = cumul + h_one * density
            if 1 <= row <= rows:
                hidden_ref[row - 1, cols, lanes] = (h_one * cumul).astype(BF16)

    for_tiles(width, dim, tile)


def back_kernel(
    edge_ref, sharp_ref, pack_ref, up_ref, near_ref, far_ref, act_mid_ref, hidden_ref, slope_ref,
    attended_ref, projected_ref, residual_ref, value_ref, act_one_ref, gain_two_ref, factor_ref,
    w_out_ref, kernel_ref,
    prob_out_ref, small_ref, d_res_ref, d_value_ref, keep_ref, give_ref,
    up_ext, d_ext, hid_ext, d_act, sums, d_proj_ref, d_att_ref, grad_ref,
):
    rows, width, dim = up_ref.shape
    head_dim = dim // sharp_ref.shape[0]
    blocks = dim // LANES
    for ref in (up_ext, d_ext, hid_ext):
        ref[:, :PAD] = jnp.zeros_like(ref[:, :PAD])
        ref[:, PAD + width :] = jnp.zeros_like(ref[:, PAD + width :])
    sums[...] = jnp.zeros_like(sums)
    main = slice(PAD, PAD + width)
    even = edge_ref[0]
    for row in range(rows):
        up_ext[EDGE + row, main, :] = up_ref[row].astype(F32)
        hid_ext[row, main, :] = hidden_ref[row].astype(F32)
    for ref, place, source in (
        (near_ref, even * (rows + EDGE), (1 - even) * (rows - EDGE)),
        (far_ref, (1 - even) * (rows + EDGE), even * (rows - EDGE)),
    ):
        for row in range(EDGE):
            up_ext[place + row, main, :] = ref[source + row].astype(F32)

    def d_hidden_tile(start, lanes):
        window = pl.ds(start, COLS + 2 * PAD)
        cols = pl.ds(start, COLS)
        factor = factor_ref[1:2, lanes]
        kernel = [kernel_ref[9 + tap : 10 + tap, lanes] * factor for tap in range(9)]
        for row in range(rows + 2):
            d_hidden = inner(row_taps(up_ext, (row, row + 1, row + 2), window, lanes, kernel, True))
            d_h = d_hidden * slope_ref[row, cols, lanes]
            if row == 0:
                d_h = jnp.where(edge_ref[1] > 0, d_h, 0.0)
            if row == rows + 1:
                d_h = jnp.where(edge_ref[2] > 0, d_h, 0.0)
            d_ext[row, pl.ds(start + PAD, COLS), lanes] = d_h

    for_tiles(width, dim, d_hidden_tile)

    def fold(value):
        return jnp.sum(value.reshape(-1, 8, LANES), 0)

    def d_act_tile(start, lanes):
        window = pl.ds(start, COLS + 2 * PAD)
        cols = pl.ds(start, COLS)
        kernel = [kernel_ref[tap : tap + 1, lanes] for tap in range(9)]
        size = COLS + 2 * PAD
        shifts = (1, 0, size - 1)
        for row in range(rows):
            d_act[row, cols, lanes] = inner(
                row_taps(d_ext, (row, row + 1, row + 2), window, lanes, kernel, True)
            )
        act = [act_mid_ref[row, cols, lanes].astype(F32) for row in range(rows + 2)]
        moved = [
            [inner(pltpu.roll(d_ext[1 + row, window, lanes], shifts[2 - j], 0)) if j != 1
             else inner(d_ext[1 + row, window, lanes]) for j in range(3)]
            for row in range(rows)
        ]
        for i in range(3):
            for j in range(3):
                total = moved[0][j] * act[i]
                for row in range(1, rows):
                    total = total + moved[row][j] * act[i + row]
                sums[3 * i + j, :, lanes] += fold(total)
        up = [up_ext[1 + row, pl.ds(start + PAD, COLS), lanes] for row in range(rows + 2)]
        moved = [
            [inner(pltpu.roll(hid_ext[row, window, lanes], shifts[j], 0)) if j != 1
             else inner(hid_ext[row, window, lanes]) for j in range(3)]
            for row in range(rows)
        ]
        for i in range(3):
            for j in range(3):
                total = moved[0][j] * up[2 - i]
                for row in range(1, rows):
                    total = total + moved[row][j] * up[2 - i + row]
                sums[9 + 3 * i + j, :, lanes] += fold(total)

    for_tiles(width, dim, d_act_tile)

    factor_one, factor_two = factor_ref[0:1, :], factor_ref[1:2, :]
    scale_one = jnp.zeros((1, dim), F32)
    step = 64
    for row in range(rows):
        for part in range(width // step):
            span = slice(row * width + part * step, row * width + (part + 1) * step)
            cols = slice(part * step, (part + 1) * step)
            normed, inverse = norm_stats(residual_ref[span, :].astype(F32))
            d_res = up_ref[row, cols, :].astype(F32) + norm_back(
                d_act[row, cols, :], gain_two_ref[...], normed, inverse
            )
            d_res_ref[span, :] = d_res
            scale_one = scale_one + jnp.sum(projected_ref[span, :] * d_res, 0, keepdims=True)
            d_proj_ref[span, :] = (factor_one * d_res).astype(BF16)
    scale_two = jnp.zeros((1, dim), F32)
    small_ref[20:, :] = jnp.zeros_like(small_ref[20:, :])
    for tap in range(9):
        small_ref[tap : tap + 1, :] = jnp.sum(sums[tap], 0, keepdims=True)
        raw = jnp.sum(sums[9 + tap], 0, keepdims=True)
        small_ref[9 + tap : 10 + tap, :] = raw * factor_two
        scale_two = scale_two + raw * kernel_ref[9 + tap : 10 + tap, :]
    small_ref[18:19, :] = scale_one
    small_ref[19:20, :] = scale_two
    d_att_ref[...] = dot32(d_proj_ref[...], w_out_ref[...], 1, 1).astype(BF16)
    for block in range(blocks):
        lanes = slice(block * LANES, (block + 1) * LANES)
        prob, *_, block_id, _ = softmax_block(pack_ref, sharp_ref, block, head_dim)
        d_att = d_att_ref[:, lanes]
        prob_out_ref[:, lanes] = compact(block_id, dot32(d_att, value_ref[:, lanes], 0, 0))
        d_value_ref[:, lanes] = dot32(d_att, block_diag(block_id, prob), 1, 0).astype(BF16)
    grad_ref[:, :dim] = dot32(act_one_ref[...], d_value_ref[...], 0, 0).astype(BF16)
    grad_ref[:, dim:] = dot32(attended_ref[...], d_proj_ref[...], 0, 0).astype(BF16)
    split_rows(grad_ref, keep_ref, give_ref, edge_ref[3])


def split_rows(full_ref, keep_ref, give_ref, bit):
    count = keep_ref.shape[0]
    size = keep_ref.shape[1]
    for index in range(count):
        for ref, side in ((keep_ref, bit), (give_ref, 1 - bit)):
            start = pl.multiple_of((2 * index + side) * size, size)
            ref[index] = full_ref[pl.ds(start, size), :]


def gram_kernel(
    edge_ref, sharp_ref, pack_ref, prob_ref, mixed_ref, act_ref, d_qk_ref, keep_ref, give_ref, grad_ref,
):
    tokens, dim = act_ref.shape
    head_dim = dim // sharp_ref.shape[0]
    for block in range(dim // LANES):
        lanes = slice(block * LANES, (block + 1) * LANES)
        key_lanes = slice(dim + block * LANES, dim + (block + 1) * LANES)
        prob, scores, sharp, divisor, query_col, key_row, block_id, diag = softmax_block(
            pack_ref, sharp_ref, block, head_dim
        )
        prob_grad = prob_ref[:, lanes]
        d_scores = prob * (prob_grad - seg_sum(block_id, prob * prob_grad))
        d_gram = block_diag(block_id, d_scores * sharp / divisor)
        weighted = d_scores * scores
        d_qsq_col = -seg_sum(block_id, weighted) / (2.0 * query_col * query_col)
        d_qsq = jnp.sum(jnp.where(diag, d_qsq_col, 0.0), 0, keepdims=True)
        d_ksq = -jnp.sum(weighted, 0, keepdims=True) / (2.0 * key_row * key_row)
        query, key = mixed_ref[:, lanes], mixed_ref[:, key_lanes]
        d_query = dot32(key, d_gram, 1, 1) + 2.0 * d_qsq * query.astype(F32)
        d_key = dot32(query, d_gram, 1, 0) + 2.0 * d_ksq * key.astype(F32)
        d_qk_ref[:, lanes] = d_query.astype(BF16)
        d_qk_ref[:, key_lanes] = d_key.astype(BF16)
    act = act_ref[...]
    for part in range(2 * dim // 256):
        cols = slice(part * 256, part * 256 + 256)
        grad_ref[:, cols] = dot32(act, d_qk_ref[:, cols], 0, 0).astype(BF16)
    split_rows(grad_ref, keep_ref, give_ref, edge_ref[3])


def input_kernel(x_ref, gain_ref, w_ref, d_qk_ref, d_value_ref, d_res_ref, out_ref):
    tokens, dim = x_ref.shape
    step = 128
    for part in range(tokens // step):
        rows = slice(part * step, (part + 1) * step)
        d_act = dot32(d_qk_ref[rows, :], w_ref[:, : 2 * dim], 1, 1) + dot32(
            d_value_ref[rows, :], w_ref[:, 2 * dim :], 1, 1
        )
        normed, inverse = norm_stats(x_ref[rows, :].astype(F32))
        out_ref[rows, :] = (
            d_res_ref[rows, :] + norm_back(d_act, gain_ref[...], normed, inverse)
        ).astype(BF16)


def call(body, name, outs, args, scalars=0, scratch=(), thirds=()):
    specs = []
    for i, arg in enumerate(args):
        if i < scalars:
            specs.append(pl.BlockSpec(memory_space=pltpu.SMEM))
        elif i in thirds:
            specs.append(pl.BlockSpec((arg.shape[0], arg.shape[1] // 3), lambda i: (0, 2)))
        else:
            specs.append(pl.BlockSpec(arg.shape, lambda i, n=arg.ndim: (0,) * n))
    return pl.pallas_call(
        body,
        name=name,
        grid=(1,),
        out_shape=[jax.ShapeDtypeStruct(shape, dtype) for shape, dtype in outs],
        in_specs=specs,
        out_specs=[pl.BlockSpec(o[0], lambda i, n=len(o[0]): (0,) * n) for o in outs],
        scratch_shapes=[pltpu.VMEM(shape, dtype) for shape, dtype in scratch],
    )(*args)


def beside(value):
    return swap_bit(value, "sp", 1)


def beyond(value):
    count = lax.axis_size("sp")
    hops = [(i, i - 2) for i in range(count) if i % 2 == 1 and i >= 2]
    hops += [(i, i + 2) for i in range(count) if i % 2 == 0 and i + 2 < count]
    return lax.ppermute(value, "sp", hops)


def after(value, earlier):
    return lax.optimization_barrier((value, earlier))


def shards(x4, up4, gain_one, w_qkv, sharp, w_out, factors, gain_two, kernels):
    rows, width, dim = x4.shape[1:]
    heads = sharp.shape[0]
    head_dim = dim // heads
    tokens = rows * width
    x_own, up_own = x4[0], up4[0]
    flat = x_own.reshape(tokens, dim)
    gain_one, gain_two = gain_one[None], gain_two[None]
    taps = kernels.reshape(-1, dim)
    index = lax.axis_index("sp")
    last = lax.axis_size("sp") - 1
    edges = jnp.stack(
        [1 - index % 2, jnp.minimum(index, 1), jnp.minimum(last - index, 1), own_bit("rep", 1)]
    )
    pack_rows = head_dim + 8

    x_near = beside(x_own)
    mixed, act_one, pack = call(
        functools.partial(first_kernel, head_dim=head_dim), "first",
        [((tokens, 3 * dim), BF16), ((tokens, dim), BF16), ((pack_rows, dim), F32)],
        (flat, gain_one, w_qkv),
    )
    sp_bits = bits_of("sp")
    for step, bit in enumerate(sp_bits):
        pack = pack + swap_bit(pack, "sp", bit)
        if step == 0:
            x_near, pack = after(x_near, pack)
            x_far = beyond(x_near)
            up_far_in, pack = after(up_own, pack)
            up_near = beside(up_far_in)
    up_near, pack = after(up_near, pack)
    up_far = beyond(up_near)
    attended, projected, residual, act_mid, hidden, slope = call(
        attend_kernel, "attend",
        [((tokens, dim), BF16), ((tokens, dim), F32), ((tokens, dim), BF16),
         ((rows + 2, width, dim), BF16), ((rows, width, dim), BF16), ((rows + 2, width, dim), F32)],
        (edges, sharp, pack, x_own, x_near, x_far, mixed, gain_one, gain_two, factors,
         w_qkv, w_out, taps),
        scalars=2,
        thirds=(6, 10),
        scratch=[((rows + 2 * EDGE, width + 2 * PAD, dim), F32), ((dim // LANES, LANES, LANES), BF16)],
    )
    blocks = lax.axis_size("rep")
    split = ((blocks // 2, dim // blocks, 2 * dim), BF16)
    prob_part, small, d_res, d_value, keep, give = call(
        back_kernel, "back",
        [((head_dim, dim), F32), ((24, dim), F32), ((tokens, dim), F32), ((tokens, dim), BF16),
         split, split],
        (edges, sharp, pack, up_own, up_near, up_far, act_mid, hidden, slope, attended, projected,
         residual, mixed, act_one, gain_two, factors, w_out, taps),
        scalars=2,
        thirds=(12,),
        scratch=[((rows + 2 * EDGE, width + 2 * PAD, dim), F32),
                 ((rows + 2, width + 2 * PAD, dim), F32), ((rows, width + 2 * PAD, dim), F32),
                 ((rows, width, dim), F32), ((18, 8, dim), F32), ((tokens, dim), BF16),
                 ((tokens, dim), BF16), ((dim, 2 * dim), BF16)],
    )
    prob_part = all_sum(prob_part, "sp")
    early = reduce_rows(keep, give)
    d_qk, keep, give = call(
        gram_kernel, "gram",
        [((tokens, 2 * dim), BF16), split, split],
        (edges, sharp, pack, prob_part, mixed, act_one), scalars=2,
        scratch=[((dim, 2 * dim), BF16)],
    )
    late = reduce_rows(keep, give)
    small = all_sum(all_sum(small, "rep"), "sp")
    (grad_input,) = call(
        input_kernel, "input", [((tokens, dim), BF16)],
        (flat, gain_one, w_qkv, d_qk, d_value, d_res),
    )
    return (
        grad_input.reshape(1, rows, width, dim),
        jnp.concatenate([late, early[:, :dim]], 1),
        early[:, dim:],
        small[:18].reshape(kernels.shape),
        small[18:20],
    )


def solution(mesh):
    rows = P("rep", "sp", None, None)
    return jax.shard_map(
        shards,
        mesh=mesh,
        in_specs=(rows, rows) + (P(),) * 7,
        out_specs=(rows, P("rep", None), P("rep", None), P(), P()),
        check_vma=False,
    )
```

```python
import functools

import jax
import jax.numpy as jnp
from jax import lax
from jax.experimental import pallas as pl
from jax.experimental.pallas import tpu as pltpu
from jax.sharding import PartitionSpec as P


EPS = 1e-06
F32 = jnp.float32
BF16 = jnp.bfloat16
LANES = 128
PAD = 8
COLS = 64
EDGE = 2


def swap_bit(value, axis, bit):
    count = lax.axis_size(axis)
    return lax.ppermute(value, axis, [(i, i ^ bit) for i in range(count)])


def bits_of(axis):
    count = lax.axis_size(axis)
    bits = []
    bit = 1
    while bit < count:
        bits.append(bit)
        bit *= 2
    return bits


def own_bit(axis, bit):
    return (lax.axis_index(axis) & bit) // bit


def add_low(parts):
    total = parts[0].astype(F32)
    for part in parts[1:]:
        total = total + part.astype(F32)
    return total.astype(BF16)


def member(axis, bits):
    return sum(own_bit(axis, bit) << place for place, bit in enumerate(bits))


def spread(bits, offset):
    return sum(bit for place, bit in enumerate(bits) if (offset >> place) & 1)


def scatter_stage(value, axis, bits, dim):
    mine = member(axis, bits)
    parts = [lax.dynamic_index_in_dim(value, mine, dim, False)]
    for offset in range(1, 1 << len(bits)):
        give = lax.dynamic_index_in_dim(value, mine ^ offset, dim, False)
        parts.append(swap_bit(give, axis, spread(bits, offset)))
    return add_low(parts)


def gather_stage(value, axis, bits):
    mine = member(axis, bits)
    parts = [value]
    for offset in range(1, 1 << len(bits)):
        parts.append(swap_bit(value, axis, spread(bits, offset)))
    out = []
    for piece in range(len(parts)):
        chosen = parts[0]
        for offset in range(1, len(parts)):
            chosen = jnp.where(mine == piece ^ offset, parts[offset], chosen)
        out.append(chosen)
    return jnp.concatenate(out)


def stages_of(axis):
    bits = bits_of(axis)
    return [bits[:1]] + [bits[i : i + 2] for i in range(1, len(bits), 2)]


def rep_rest(value, bits):
    cols = value.shape[-1]
    for bit in bits:
        value = value.reshape(-1, 2, value.shape[-2], cols)
        value = scatter_stage(value, "rep", [bit], 1)
    return value.reshape(-1, cols)


def sp_rows(value):
    cols = value.shape[-1]
    for bits in stages_of("sp"):
        value = scatter_stage(value.reshape(1 << len(bits), -1, cols), "sp", bits, 0)
    for bits in reversed(stages_of("sp")):
        value = gather_stage(value, "sp", bits)
    return value.astype(F32)


def dot32(a, b, left, right):
    return lax.dot_general(a, b, (((left,), (right,)), ((), ())), preferred_element_type=F32)


def norm_stats(values):
    centred = values - jnp.mean(values, -1, keepdims=True)
    inverse = lax.rsqrt(jnp.mean(centred * centred, -1, keepdims=True) + EPS)
    return centred * inverse, inverse


def norm_back(upstream, gain_vec, normed, inverse):
    scaled = upstream * gain_vec
    return inverse * (
        scaled
        - jnp.mean(scaled, -1, keepdims=True)
        - normed * jnp.mean(scaled * normed, -1, keepdims=True)
    )


def masks(head_dim):
    lane = lax.broadcasted_iota(jnp.int32, (head_dim, LANES), 1)
    row = lax.broadcasted_iota(jnp.int32, (head_dim, LANES), 0)
    return lane // head_dim, lane % head_dim == row


def by_head(block_id, parts):
    out = parts[-1]
    for index in range(len(parts) - 2, -1, -1):
        out = jnp.where(block_id == index, parts[index], out)
    return out


def seg_reduce(block_id, value, fill, func):
    count = LANES // value.shape[0]
    parts = [
        func(jnp.where(block_id == index, value, fill), -1, keepdims=True) for index in range(count)
    ]
    return by_head(block_id, parts)


def seg_sum(block_id, value):
    return seg_reduce(block_id, value, 0.0, jnp.sum)


def block_diag(block_id, value):
    count = LANES // value.shape[0]
    return jnp.concatenate(
        [jnp.where(block_id == index, value, 0.0) for index in range(count)], 0
    ).astype(BF16)


def compact(block_id, full):
    head_dim = block_id.shape[0]
    count = LANES // head_dim
    return by_head(block_id, [full[i * head_dim : (i + 1) * head_dim] for i in range(count)])


def softmax_block(pack_ref, sharp_ref, block, head_dim):
    block_id, diag = masks(head_dim)
    lanes = slice(block * LANES, (block + 1) * LANES)
    count = LANES // head_dim
    gram = pack_ref[:head_dim, lanes]
    query_row = jnp.sqrt(pack_ref[head_dim : head_dim + 1, lanes] + EPS)
    key_row = jnp.sqrt(pack_ref[head_dim + 1 : head_dim + 2, lanes] + EPS)
    query_col = seg_sum(block_id, jnp.where(diag, query_row, 0.0))
    sharp = by_head(block_id, [sharp_ref[block * count + i] for i in range(count)])
    divisor = query_col * key_row
    scores = sharp * gram / divisor
    shifted = scores - seg_reduce(block_id, scores, -jnp.inf, jnp.max)
    exponent = jnp.exp(shifted)
    prob = exponent / seg_sum(block_id, exponent)
    return prob, scores, sharp, divisor, query_col, key_row, block_id, diag


def first_kernel(x_ref, gain_ref, w_ref, mixed_ref, act_ref, pack_ref, *, head_dim):
    tokens, dim = x_ref.shape
    step = 64

    @pl.loop(0, tokens // step)
    def _(index):
        rows = pl.ds(pl.multiple_of(index * step, step), step)
        normed, _ = norm_stats(x_ref[rows, :].astype(F32))
        act_ref[rows, :] = (normed * gain_ref[...]).astype(BF16)

    act = act_ref[...]
    for part in range(w_ref.shape[1] // 256):
        cols = slice(part * 256, part * 256 + 256)
        mixed_ref[:, cols] = dot32(act, w_ref[:, cols], 1, 0).astype(BF16)
    block_id, _ = masks(head_dim)
    pack_ref[head_dim:, :] = jnp.zeros_like(pack_ref[head_dim:, :])
    for block in range(dim // LANES):
        lanes = slice(block * LANES, (block + 1) * LANES)
        query = mixed_ref[:, lanes]
        key = mixed_ref[:, dim + block * LANES : dim + (block + 1) * LANES]
        pack_ref[:head_dim, lanes] = compact(block_id, dot32(query, key, 0, 0))
        for row, value in enumerate((query, key)):
            value = value.astype(F32)
            pack_ref[head_dim + row : head_dim + row + 1, lanes] = jnp.sum(
                value * value, 0, keepdims=True
            )


def shift_sum(parts):
    size = parts[1].shape[0]
    return pltpu.roll(parts[0], 1, 0) + parts[1] + pltpu.roll(parts[2], size - 1, 0)


def inner(value):
    return value[PAD:-PAD]


def row_taps(ref, rows, window, lanes, kernel, flip):
    loaded = [ref[row, window, lanes] for row in rows]
    parts = []
    for j in range(3):
        total = None
        for i in range(3):
            tap = kernel[3 * i + j]
            term = loaded[2 - i if flip else i] * tap
            total = term if total is None else total + term
        parts.append(total)
    return shift_sum(parts[::-1] if flip else parts)


def for_tiles(width, dim, body):
    @pl.loop(0, dim // LANES)
    def _(block):
        lanes = pl.ds(pl.multiple_of(block * LANES, LANES), LANES)

        @pl.loop(0, width // COLS)
        def _(part):
            start = pl.multiple_of(part * COLS, COLS)
            body(start, lanes)


def attend_kernel(
    edge_ref, sharp_ref, pack_ref, x_ref, near_ref, far_ref, value_ref, gain_one_ref, gain_two_ref,
    factor_ref, w_value_ref, w_out_ref, kernel_ref,
    attended_ref, projected_ref, residual_ref, act_mid_ref, hidden_ref, slope_ref, act_ext, diag_ref,
):
    rows, width, dim = x_ref.shape
    head_dim = dim // sharp_ref.shape[0]
    blocks = dim // LANES
    for block in range(blocks):
        prob, *_, block_id, _ = softmax_block(pack_ref, sharp_ref, block, head_dim)
        diag_ref[block] = block_diag(block_id, prob)
    act_ext[:, :PAD] = jnp.zeros_like(act_ext[:, :PAD])
    act_ext[:, PAD + width :] = jnp.zeros_like(act_ext[:, PAD + width :])

    def token_part(x_rows, value, place, own):
        parts = []
        for block in range(blocks):
            lanes = slice(block * LANES, (block + 1) * LANES)
            parts.append(dot32(value[:, lanes], diag_ref[block], 1, 1).astype(BF16))
        attended = jnp.concatenate(parts, 1)
        projected = dot32(attended, w_out_ref[...], 1, 0)
        residual = (x_rows + factor_ref[0:1, :] * projected).astype(BF16)
        normed, _ = norm_stats(residual.astype(F32))
        act = (normed * gain_two_ref[...]).astype(BF16)
        act_ext[place, PAD : PAD + width, :] = act.astype(F32)
        if own is not None:
            span = slice(own * width, (own + 1) * width)
            attended_ref[span, :] = attended
            projected_ref[span, :] = projected
            residual_ref[span, :] = residual

    for row in range(rows):
        value = value_ref[row * width : (row + 1) * width, :]
        token_part(x_ref[row].astype(F32), value, EDGE + row, row)
    even = edge_ref[0]
    for ref, place, source in (
        (near_ref, even * (rows + EDGE), (1 - even) * (rows - EDGE)),
        (far_ref, (1 - even) * (rows + EDGE), even * (rows - EDGE)),
    ):
        for row in range(EDGE):
            x_rows = ref[source + row].astype(F32)
            normed, _ = norm_stats(x_rows)
            act = (normed * gain_one_ref[...]).astype(BF16)
            value = dot32(act, w_value_ref[...], 1, 0).astype(BF16)
            token_part(x_rows, value, place + row, None)
    for row in range(rows + 2):
        act_mid_ref[row] = act_ext[row + 1, PAD : PAD + width, :].astype(BF16)

    def tile(start, lanes):
        window = pl.ds(start, COLS + 2 * PAD)
        cols = pl.ds(start, COLS)
        kernel = [kernel_ref[tap : tap + 1, lanes] for tap in range(9)]
        for row in range(rows + 2):
            h_one = inner(row_taps(act_ext, (row, row + 1, row + 2), window, lanes, kernel, False))
            cumul = 0.5 * (1.0 + lax.erf(h_one * 0.7071067811865476))
            density = jnp.exp(-0.5 * h_one * h_one) * 0.3989422804014327
            slope_ref[row, cols, lanes] = cumul + h_one * density
            if 1 <= row <= rows:
                hidden_ref[row - 1, cols, lanes] = (h_one * cumul).astype(BF16)

    for_tiles(width, dim, tile)


def back_kernel(
    edge_ref, sharp_ref, pack_ref, up_ref, near_ref, far_ref, act_mid_ref, hidden_ref, slope_ref,
    attended_ref, projected_ref, residual_ref, value_ref, act_one_ref, gain_two_ref, factor_ref,
    w_out_ref, kernel_ref,
    prob_out_ref, d_res_ref, d_value_ref, keep_ref, give_ref,
    up_ext, d_ext, hid_ext, d_act, sums, d_proj_ref, d_att_ref, grad_ref,
):
    rows, width, dim = up_ref.shape
    head_dim = dim // sharp_ref.shape[0]
    blocks = dim // LANES
    for ref in (up_ext, d_ext, hid_ext):
        ref[:, :PAD] = jnp.zeros_like(ref[:, :PAD])
        ref[:, PAD + width :] = jnp.zeros_like(ref[:, PAD + width :])
    sums[...] = jnp.zeros_like(sums)
    main = slice(PAD, PAD + width)
    even = edge_ref[0]
    for row in range(rows):
        up_ext[EDGE + row, main, :] = up_ref[row].astype(F32)
        hid_ext[row, main, :] = hidden_ref[row].astype(F32)
    for ref, place, source in (
        (near_ref, even * (rows + EDGE), (1 - even) * (rows - EDGE)),
        (far_ref, (1 - even) * (rows + EDGE), even * (rows - EDGE)),
    ):
        for row in range(EDGE):
            up_ext[place + row, main, :] = ref[source + row].astype(F32)

    def d_hidden_tile(start, lanes):
        window = pl.ds(start, COLS + 2 * PAD)
        cols = pl.ds(start, COLS)
        factor = factor_ref[1:2, lanes]
        kernel = [kernel_ref[9 + tap : 10 + tap, lanes] * factor for tap in range(9)]
        for row in range(rows + 2):
            d_hidden = inner(row_taps(up_ext, (row, row + 1, row + 2), window, lanes, kernel, True))
            d_h = d_hidden * slope_ref[row, cols, lanes]
            if row == 0:
                d_h = jnp.where(edge_ref[1] > 0, d_h, 0.0)
            if row == rows + 1:
                d_h = jnp.where(edge_ref[2] > 0, d_h, 0.0)
            d_ext[row, pl.ds(start + PAD, COLS), lanes] = d_h

    for_tiles(width, dim, d_hidden_tile)

    def fold(value):
        return jnp.sum(value.reshape(-1, 8, LANES), 0)

    def d_act_tile(start, lanes):
        window = pl.ds(start, COLS + 2 * PAD)
        cols = pl.ds(start, COLS)
        kernel = [kernel_ref[tap : tap + 1, lanes] for tap in range(9)]
        size = COLS + 2 * PAD
        shifts = (1, 0, size - 1)
        for row in range(rows):
            d_act[row, cols, lanes] = inner(
                row_taps(d_ext, (row, row + 1, row + 2), window, lanes, kernel, True)
            )
        act = [act_mid_ref[row, cols, lanes].astype(F32) for row in range(rows + 2)]
        moved = [
            [inner(pltpu.roll(d_ext[1 + row, window, lanes], shifts[2 - j], 0)) if j != 1
             else inner(d_ext[1 + row, window, lanes]) for j in range(3)]
            for row in range(rows)
        ]
        for i in range(3):
            for j in range(3):
                total = moved[0][j] * act[i]
                for row in range(1, rows):
                    total = total + moved[row][j] * act[i + row]
                sums[3 * i + j, :, lanes] += fold(total)
        up = [up_ext[1 + row, pl.ds(start + PAD, COLS), lanes] for row in range(rows + 2)]
        moved = [
            [inner(pltpu.roll(hid_ext[row, window, lanes], shifts[j], 0)) if j != 1
             else inner(hid_ext[row, window, lanes]) for j in range(3)]
            for row in range(rows)
        ]
        for i in range(3):
            for j in range(3):
                total = moved[0][j] * up[2 - i]
                for row in range(1, rows):
                    total = total + moved[row][j] * up[2 - i + row]
                sums[9 + 3 * i + j, :, lanes] += fold(total)

    for_tiles(width, dim, d_act_tile)

    factor_one, factor_two = factor_ref[0:1, :], factor_ref[1:2, :]
    scale_one = jnp.zeros((1, dim), F32)
    step = 64
    for row in range(rows):
        for part in range(width // step):
            span = slice(row * width + part * step, row * width + (part + 1) * step)
            cols = slice(part * step, (part + 1) * step)
            normed, inverse = norm_stats(residual_ref[span, :].astype(F32))
            d_res = up_ref[row, cols, :].astype(F32) + norm_back(
                d_act[row, cols, :], gain_two_ref[...], normed, inverse
            )
            d_res_ref[span, :] = d_res
            scale_one = scale_one + jnp.sum(projected_ref[span, :] * d_res, 0, keepdims=True)
            d_proj_ref[span, :] = (factor_one * d_res).astype(BF16)
    scale_two = jnp.zeros((1, dim), F32)
    small_ref = prob_out_ref.at[head_dim:]
    small_ref[20:, :] = jnp.zeros((4, dim), F32)
    for tap in range(9):
        small_ref[tap : tap + 1, :] = jnp.sum(sums[tap], 0, keepdims=True)
        raw = jnp.sum(sums[9 + tap], 0, keepdims=True)
        small_ref[9 + tap : 10 + tap, :] = raw * factor_two
        scale_two = scale_two + raw * kernel_ref[9 + tap : 10 + tap, :]
    small_ref[18:19, :] = scale_one
    small_ref[19:20, :] = scale_two
    d_att_ref[...] = dot32(d_proj_ref[...], w_out_ref[...], 1, 1).astype(BF16)
    for block in range(blocks):
        lanes = slice(block * LANES, (block + 1) * LANES)
        prob, *_, block_id, _ = softmax_block(pack_ref, sharp_ref, block, head_dim)
        d_att = d_att_ref[:, lanes]
        prob_out_ref[:head_dim, lanes] = compact(block_id, dot32(d_att, value_ref[:, lanes], 0, 0))
        d_value_ref[:, lanes] = dot32(d_att, block_diag(block_id, prob), 1, 0).astype(BF16)
    grad_ref[:, :dim] = dot32(act_one_ref[...], d_value_ref[...], 0, 0).astype(BF16)
    grad_ref[:, dim:] = dot32(attended_ref[...], d_proj_ref[...], 0, 0).astype(BF16)
    split_rows(grad_ref, keep_ref, give_ref, edge_ref[3])


def split_rows(full_ref, keep_ref, give_ref, bit):
    count = keep_ref.shape[0]
    size = keep_ref.shape[1]
    for index in range(count):
        for ref, side in ((keep_ref, bit), (give_ref, 1 - bit)):
            start = pl.multiple_of((2 * index + side) * size, size)
            ref[index] = full_ref[pl.ds(start, size), :]


def gram_kernel(
    edge_ref, sharp_ref, pack_ref, prob_ref, mixed_ref, act_ref, d_qk_ref, keep_ref, give_ref, grad_ref,
):
    _, dim = act_ref.shape
    head_dim = dim // sharp_ref.shape[0]
    for block in range(dim // LANES):
        lanes = slice(block * LANES, (block + 1) * LANES)
        key_lanes = slice(dim + block * LANES, dim + (block + 1) * LANES)
        prob, scores, sharp, divisor, query_col, key_row, block_id, diag = softmax_block(
            pack_ref, sharp_ref, block, head_dim
        )
        prob_grad = prob_ref[:head_dim, lanes]
        d_scores = prob * (prob_grad - seg_sum(block_id, prob * prob_grad))
        d_gram = block_diag(block_id, d_scores * sharp / divisor)
        weighted = d_scores * scores
        d_qsq_col = -seg_sum(block_id, weighted) / (2.0 * query_col * query_col)
        d_qsq = jnp.sum(jnp.where(diag, d_qsq_col, 0.0), 0, keepdims=True)
        d_ksq = -jnp.sum(weighted, 0, keepdims=True) / (2.0 * key_row * key_row)
        query, key = mixed_ref[:, lanes], mixed_ref[:, key_lanes]
        d_query = dot32(key, d_gram, 1, 1) + 2.0 * d_qsq * query.astype(F32)
        d_key = dot32(query, d_gram, 1, 0) + 2.0 * d_ksq * key.astype(F32)
        d_qk_ref[:, lanes] = d_query.astype(BF16)
        d_qk_ref[:, key_lanes] = d_key.astype(BF16)
    act = act_ref[...]
    for part in range(2 * dim // 256):
        cols = slice(part * 256, part * 256 + 256)
        grad_ref[:, cols] = dot32(act, d_qk_ref[:, cols], 0, 0).astype(BF16)
    split_rows(grad_ref, keep_ref, give_ref, edge_ref[3])


def input_kernel(x_ref, gain_ref, w_ref, d_qk_ref, d_value_ref, d_res_ref, out_ref):
    tokens, dim = x_ref.shape
    step = 128
    for part in range(tokens // step):
        rows = slice(part * step, (part + 1) * step)
        d_act = dot32(d_qk_ref[rows, :], w_ref[:, : 2 * dim], 1, 1) + dot32(
            d_value_ref[rows, :], w_ref[:, 2 * dim :], 1, 1
        )
        normed, inverse = norm_stats(x_ref[rows, :].astype(F32))
        out_ref[rows, :] = (
            d_res_ref[rows, :] + norm_back(d_act, gain_ref[...], normed, inverse)
        ).astype(BF16)


def call(body, outs, args, scalars=0, scratch=(), thirds=()):
    specs = []
    for i, arg in enumerate(args):
        if i < scalars:
            specs.append(pl.BlockSpec(memory_space=pltpu.SMEM))
        elif i in thirds:
            specs.append(pl.BlockSpec((arg.shape[0], arg.shape[1] // 3), lambda i: (0, 2)))
        else:
            specs.append(pl.BlockSpec(arg.shape, lambda i, n=arg.ndim: (0,) * n))
    return pl.pallas_call(
        body,
        grid=(1,),
        out_shape=[jax.ShapeDtypeStruct(shape, dtype) for shape, dtype in outs],
        in_specs=specs,
        out_specs=[pl.BlockSpec(o[0], lambda i, n=len(o[0]): (0,) * n) for o in outs],
        scratch_shapes=[pltpu.VMEM(shape, dtype) for shape, dtype in scratch],
    )(*args)


def beside(value):
    return swap_bit(value, "sp", 1)


def beyond(value):
    count = lax.axis_size("sp")
    hops = [(i, i - 2) for i in range(count) if i % 2 == 1 and i >= 2]
    hops += [(i, i + 2) for i in range(count) if i % 2 == 0 and i + 2 < count]
    return lax.ppermute(value, "sp", hops)


def after(value, *earlier):
    return lax.optimization_barrier((value, *earlier))[0]


def shards(x4, up4, gain_one, w_qkv, sharp, w_out, factors, gain_two, kernels):
    rows, width, dim = x4.shape[1:]
    heads = sharp.shape[0]
    head_dim = dim // heads
    tokens = rows * width
    x_own, up_own = x4[0], up4[0]
    flat = x_own.reshape(tokens, dim)
    gain_one, gain_two = gain_one[None], gain_two[None]
    taps = kernels.reshape(-1, dim)
    index = lax.axis_index("sp")
    last = lax.axis_size("sp") - 1
    edges = jnp.stack(
        [1 - index % 2, jnp.minimum(index, 1), jnp.minimum(last - index, 1), own_bit("rep", 1)]
    )
    pack_rows = head_dim + 8
    sp_bits = bits_of("sp")
    sp_bits = sp_bits[1:] + sp_bits[:1]

    x_near = beside(x_own)
    mixed, act_one, pack = call(
        functools.partial(first_kernel, head_dim=head_dim),
        [((tokens, 3 * dim), BF16), ((tokens, dim), BF16), ((pack_rows, dim), F32)],
        (flat, gain_one, w_qkv),
    )
    up_near = beside(after(up_own, pack))
    packs = [pack]
    for bit in sp_bits:
        packs.append(packs[-1] + swap_bit(packs[-1], "sp", bit))
    x_far = beyond(after(x_near, packs[1]))
    up_far = beyond(after(up_near, packs[-2]))
    pack = packs[-1]
    attended, projected, residual, act_mid, hidden, slope = call(
        attend_kernel,
        [((tokens, dim), BF16), ((tokens, dim), F32), ((tokens, dim), BF16),
         ((rows + 2, width, dim), BF16), ((rows, width, dim), BF16), ((rows + 2, width, dim), F32)],
        (edges, sharp, pack, x_own, x_near, x_far, mixed, gain_one, gain_two, factors,
         w_qkv, w_out, taps),
        scalars=2,
        thirds=(6, 10),
        scratch=[((rows + 2 * EDGE, width + 2 * PAD, dim), F32), ((dim // LANES, LANES, LANES), BF16)],
    )
    blocks = lax.axis_size("rep")
    split = ((blocks // 2, dim // blocks, 2 * dim), BF16)
    prob_part, d_res, d_value, keep, give = call(
        back_kernel,
        [((head_dim + 24, dim), F32), ((tokens, dim), F32), ((tokens, dim), BF16), split, split],
        (edges, sharp, pack, up_own, up_near, up_far, act_mid, hidden, slope, attended, projected,
         residual, mixed, act_one, gain_two, factors, w_out, taps),
        scalars=2,
        thirds=(12,),
        scratch=[((rows + 2 * EDGE, width + 2 * PAD, dim), F32),
                 ((rows + 2, width + 2 * PAD, dim), F32), ((rows, width + 2 * PAD, dim), F32),
                 ((rows, width, dim), F32), ((18, 8, dim), F32), ((tokens, dim), BF16),
                 ((tokens, dim), BF16), ((dim, 2 * dim), BF16)],
    )
    probs = [prob_part]
    for bit in sp_bits:
        probs.append(probs[-1] + swap_bit(probs[-1], "sp", bit))
    prob_part = probs[-1]
    d_qk, late_keep, late_give = call(
        gram_kernel,
        [((tokens, 2 * dim), BF16), split, split],
        (edges, sharp, pack, prob_part, mixed, act_one), scalars=2,
        scratch=[((dim, 2 * dim), BF16)],
    )
    rep_bits = bits_of("rep")

    early = add_low([keep, swap_bit(give, "rep", rep_bits[0])])
    early = rep_rest(early, rep_bits[1:])

    late = add_low([late_keep, swap_bit(late_give, "rep", rep_bits[0])])
    late = rep_rest(late, rep_bits[1:])
    both = jnp.concatenate([late, early], -1)
    both = sp_rows(both)

    small = prob_part[head_dim:]
    small = small + swap_bit(after(small, d_qk), "rep", rep_bits[0])
    for bit in rep_bits[1:]:
        small = small + swap_bit(small, "rep", bit)
    (grad_input,) = call(
        input_kernel, [((tokens, dim), BF16)],
        (flat, gain_one, w_qkv, d_qk, d_value, d_res),
    )
    return (
        grad_input.reshape(1, rows, width, dim),
        both[:, : 3 * dim],
        both[:, 3 * dim :],
        small[:18].reshape(kernels.shape),
        small[18:20],
    )


def solution(mesh):
    rows = P("rep", "sp", None, None)
    return jax.shard_map(
        shards,
        mesh=mesh,
        in_specs=(rows, rows) + (P(),) * 7,
        out_specs=(rows, P("rep", None), P("rep", None), P(), P()),
        check_vma=False,
    )
```

```python
import functools

import jax
import jax.numpy as jnp
from jax import lax
from jax.experimental import pallas as pl
from jax.experimental.pallas import tpu as pltpu
from jax.sharding import PartitionSpec as P


EPS = 1e-06
F32 = jnp.float32
BF16 = jnp.bfloat16
LANES = 128
PAD = 8
COLS = 64
EDGE = 2


def swap_bit(value, axis, bit):
    count = lax.axis_size(axis)
    return lax.ppermute(value, axis, [(i, i ^ bit) for i in range(count)])


def bits_of(axis):
    count = lax.axis_size(axis)
    bits = []
    bit = 1
    while bit < count:
        bits.append(bit)
        bit *= 2
    return bits


def own_bit(axis, bit):
    return (lax.axis_index(axis) & bit) // bit


def add_low(parts):
    total = parts[0].astype(F32)
    for part in parts[1:]:
        total = total + part.astype(F32)
    return total.astype(BF16)


def member(axis, bits):
    return sum(own_bit(axis, bit) << place for place, bit in enumerate(bits))


def spread(bits, offset):
    return sum(bit for place, bit in enumerate(bits) if (offset >> place) & 1)


def scatter_stage(value, axis, bits, dim):
    mine = member(axis, bits)
    parts = [lax.dynamic_index_in_dim(value, mine, dim, False)]
    for offset in range(1, 1 << len(bits)):
        give = lax.dynamic_index_in_dim(value, mine ^ offset, dim, False)
        parts.append(swap_bit(give, axis, spread(bits, offset)))
    return add_low(parts)


def gather_stage(value, axis, bits):
    mine = member(axis, bits)
    parts = [value]
    for offset in range(1, 1 << len(bits)):
        parts.append(swap_bit(value, axis, spread(bits, offset)))
    out = []
    for piece in range(len(parts)):
        chosen = parts[0]
        for offset in range(1, len(parts)):
            chosen = jnp.where(mine == piece ^ offset, parts[offset], chosen)
        out.append(chosen)
    return jnp.concatenate(out)


def stages_of(axis):
    bits = bits_of(axis)
    return [bits[:1]] + [bits[i : i + 2] for i in range(1, len(bits), 2)]


def rep_rest(value, bits):
    cols = value.shape[-1]
    for bit in bits:
        value = value.reshape(-1, 2, value.shape[-2], cols)
        value = scatter_stage(value, "rep", [bit], 1)
    return value.reshape(-1, cols)


def sp_rows(value):
    cols = value.shape[-1]
    for bits in stages_of("sp"):
        value = scatter_stage(value.reshape(1 << len(bits), -1, cols), "sp", bits, 0)
    for bits in reversed(stages_of("sp")):
        value = gather_stage(value, "sp", bits)
    return value.astype(F32)


def dot32(a, b, left, right):
    return lax.dot_general(a, b, (((left,), (right,)), ((), ())), preferred_element_type=F32)


def norm_stats(values):
    centred = values - jnp.mean(values, -1, keepdims=True)
    inverse = lax.rsqrt(jnp.mean(centred * centred, -1, keepdims=True) + EPS)
    return centred * inverse, inverse


def norm_back(upstream, gain_vec, normed, inverse):
    scaled = upstream * gain_vec
    return inverse * (
        scaled
        - jnp.mean(scaled, -1, keepdims=True)
        - normed * jnp.mean(scaled * normed, -1, keepdims=True)
    )


def masks(head_dim):
    lane = lax.broadcasted_iota(jnp.int32, (head_dim, LANES), 1)
    row = lax.broadcasted_iota(jnp.int32, (head_dim, LANES), 0)
    return lane // head_dim, lane % head_dim == row


def by_head(block_id, parts):
    out = parts[-1]
    for index in range(len(parts) - 2, -1, -1):
        out = jnp.where(block_id == index, parts[index], out)
    return out


def seg_reduce(block_id, value, fill, func):
    count = LANES // value.shape[0]
    parts = [
        func(jnp.where(block_id == index, value, fill), -1, keepdims=True) for index in range(count)
    ]
    return by_head(block_id, parts)


def seg_sum(block_id, value):
    return seg_reduce(block_id, value, 0.0, jnp.sum)


def block_diag(block_id, value):
    count = LANES // value.shape[0]
    return jnp.concatenate(
        [jnp.where(block_id == index, value, 0.0) for index in range(count)], 0
    ).astype(BF16)


def compact(block_id, full):
    head_dim = block_id.shape[0]
    count = LANES // head_dim
    return by_head(block_id, [full[i * head_dim : (i + 1) * head_dim] for i in range(count)])


def softmax_block(pack_ref, sharp_ref, block, head_dim):
    block_id, diag = masks(head_dim)
    lanes = slice(block * LANES, (block + 1) * LANES)
    count = LANES // head_dim
    gram = pack_ref[:head_dim, lanes]
    query_row = jnp.sqrt(pack_ref[head_dim : head_dim + 1, lanes] + EPS)
    key_row = jnp.sqrt(pack_ref[head_dim + 1 : head_dim + 2, lanes] + EPS)
    query_col = seg_sum(block_id, jnp.where(diag, query_row, 0.0))
    sharp = by_head(block_id, [sharp_ref[block * count + i] for i in range(count)])
    divisor = query_col * key_row
    scores = sharp * gram / divisor
    shifted = scores - seg_reduce(block_id, scores, -jnp.inf, jnp.max)
    exponent = jnp.exp(shifted)
    prob = exponent / seg_sum(block_id, exponent)
    return prob, scores, sharp, divisor, query_col, key_row, block_id, diag


def first_kernel(x_ref, gain_ref, w_ref, mixed_ref, act_ref, pack_ref, *, head_dim):
    tokens, dim = x_ref.shape
    step = 64

    @pl.loop(0, tokens // step)
    def _(index):
        rows = pl.ds(pl.multiple_of(index * step, step), step)
        normed, _ = norm_stats(x_ref[rows, :].astype(F32))
        act_ref[rows, :] = (normed * gain_ref[...]).astype(BF16)

    act = act_ref[...]
    for part in range(w_ref.shape[1] // 256):
        cols = slice(part * 256, part * 256 + 256)
        mixed_ref[:, cols] = dot32(act, w_ref[:, cols], 1, 0).astype(BF16)
    block_id, _ = masks(head_dim)
    pack_ref[head_dim:, :] = jnp.zeros_like(pack_ref[head_dim:, :])
    for block in range(dim // LANES):
        lanes = slice(block * LANES, (block + 1) * LANES)
        query = mixed_ref[:, lanes]
        key = mixed_ref[:, dim + block * LANES : dim + (block + 1) * LANES]
        pack_ref[:head_dim, lanes] = compact(block_id, dot32(query, key, 0, 0))
        for row, value in enumerate((query, key)):
            value = value.astype(F32)
            pack_ref[head_dim + row : head_dim + row + 1, lanes] = jnp.sum(
                value * value, 0, keepdims=True
            )


def shift_sum(parts):
    size = parts[1].shape[0]
    return pltpu.roll(parts[0], 1, 0) + parts[1] + pltpu.roll(parts[2], size - 1, 0)


def inner(value):
    return value[PAD:-PAD]


def row_taps(ref, rows, window, lanes, kernel, flip):
    loaded = [ref[row, window, lanes] for row in rows]
    parts = []
    for j in range(3):
        total = None
        for i in range(3):
            tap = kernel[3 * i + j]
            term = loaded[2 - i if flip else i] * tap
            total = term if total is None else total + term
        parts.append(total)
    return shift_sum(parts[::-1] if flip else parts)


def for_tiles(width, dim, body):
    @pl.loop(0, dim // LANES)
    def _(block):
        lanes = pl.ds(pl.multiple_of(block * LANES, LANES), LANES)

        @pl.loop(0, width // COLS)
        def _(part):
            start = pl.multiple_of(part * COLS, COLS)
            body(start, lanes)


def attend_kernel(
    edge_ref, sharp_ref, pack_ref, x_ref, near_ref, far_ref, mixed_ref, gain_one_ref, gain_two_ref,
    factor_ref, w_qkv_ref, w_out_ref, kernel_ref,
    attended_ref, projected_ref, residual_ref, act_mid_ref, hidden_ref, slope_ref, act_ext, diag_ref,
):
    rows, width, dim = x_ref.shape
    head_dim = dim // sharp_ref.shape[0]
    blocks = dim // LANES
    for block in range(blocks):
        prob, *_, block_id, _ = softmax_block(pack_ref, sharp_ref, block, head_dim)
        diag_ref[block] = block_diag(block_id, prob)
    act_ext[:, :PAD] = jnp.zeros_like(act_ext[:, :PAD])
    act_ext[:, PAD + width :] = jnp.zeros_like(act_ext[:, PAD + width :])

    def token_part(x_rows, value, place, own):
        parts = []
        for block in range(blocks):
            lanes = slice(block * LANES, (block + 1) * LANES)
            parts.append(dot32(value[:, lanes], diag_ref[block], 1, 1).astype(BF16))
        attended = jnp.concatenate(parts, 1)
        projected = dot32(attended, w_out_ref[...], 1, 0)
        residual = (x_rows + factor_ref[0:1, :] * projected).astype(BF16)
        normed, _ = norm_stats(residual.astype(F32))
        act = (normed * gain_two_ref[...]).astype(BF16)
        act_ext[place, PAD : PAD + width, :] = act.astype(F32)
        if own is not None:
            span = slice(own * width, (own + 1) * width)
            attended_ref[span, :] = attended
            projected_ref[span, :] = projected
            residual_ref[span, :] = residual

    for row in range(rows):
        value = mixed_ref[row * width : (row + 1) * width, 2 * dim :]
        token_part(x_ref[row].astype(F32), value, EDGE + row, row)
    even = edge_ref[0]
    for ref, place, source in (
        (near_ref, even * (rows + EDGE), (1 - even) * (rows - EDGE)),
        (far_ref, (1 - even) * (rows + EDGE), even * (rows - EDGE)),
    ):
        for row in range(EDGE):
            x_rows = ref[source + row].astype(F32)
            normed, _ = norm_stats(x_rows)
            act = (normed * gain_one_ref[...]).astype(BF16)
            value = dot32(act, w_qkv_ref[:, 2 * dim :], 1, 0).astype(BF16)
            token_part(x_rows, value, place + row, None)
    for row in range(rows + 2):
        act_mid_ref[row] = act_ext[row + 1, PAD : PAD + width, :].astype(BF16)

    def tile(start, lanes):
        window = pl.ds(start, COLS + 2 * PAD)
        cols = pl.ds(start, COLS)
        kernel = [kernel_ref[tap : tap + 1, lanes] for tap in range(9)]
        for row in range(rows + 2):
            h_one = inner(row_taps(act_ext, (row, row + 1, row + 2), window, lanes, kernel, False))
            cumul = 0.5 * (1.0 + lax.erf(h_one * 0.7071067811865476))
            density = jnp.exp(-0.5 * h_one * h_one) * 0.3989422804014327
            slope_ref[row, cols, lanes] = cumul + h_one * density
            if 1 <= row <= rows:
                hidden_ref[row - 1, cols, lanes] = (h_one * cumul).astype(BF16)

    for_tiles(width, dim, tile)


def back_kernel(
    edge_ref, sharp_ref, pack_ref, up_ref, near_ref, far_ref, act_mid_ref, hidden_ref, slope_ref,
    attended_ref, projected_ref, residual_ref, mixed_ref, act_one_ref, gain_two_ref, factor_ref,
    w_out_ref, kernel_ref,
    prob_out_ref, d_res_ref, d_value_ref, keep_ref, give_ref,
    up_ext, d_ext, hid_ext, d_act, sums, d_proj_ref, d_att_ref, grad_ref,
):
    rows, width, dim = up_ref.shape
    head_dim = dim // sharp_ref.shape[0]
    blocks = dim // LANES
    for ref in (up_ext, d_ext, hid_ext):
        ref[:, :PAD] = jnp.zeros_like(ref[:, :PAD])
        ref[:, PAD + width :] = jnp.zeros_like(ref[:, PAD + width :])
    sums[...] = jnp.zeros_like(sums)
    main = slice(PAD, PAD + width)
    even = edge_ref[0]
    for row in range(rows):
        up_ext[EDGE + row, main, :] = up_ref[row].astype(F32)
        hid_ext[row, main, :] = hidden_ref[row].astype(F32)
    for ref, place, source in (
        (near_ref, even * (rows + EDGE), (1 - even) * (rows - EDGE)),
        (far_ref, (1 - even) * (rows + EDGE), even * (rows - EDGE)),
    ):
        for row in range(EDGE):
            up_ext[place + row, main, :] = ref[source + row].astype(F32)

    def d_hidden_tile(start, lanes):
        window = pl.ds(start, COLS + 2 * PAD)
        cols = pl.ds(start, COLS)
        factor = factor_ref[1:2, lanes]
        kernel = [kernel_ref[9 + tap : 10 + tap, lanes] * factor for tap in range(9)]
        for row in range(rows + 2):
            d_hidden = inner(row_taps(up_ext, (row, row + 1, row + 2), window, lanes, kernel, True))
            d_h = d_hidden * slope_ref[row, cols, lanes]
            if row == 0:
                d_h = jnp.where(edge_ref[1] > 0, d_h, 0.0)
            if row == rows + 1:
                d_h = jnp.where(edge_ref[2] > 0, d_h, 0.0)
            d_ext[row, pl.ds(start + PAD, COLS), lanes] = d_h

    for_tiles(width, dim, d_hidden_tile)

    def fold(value):
        return jnp.sum(value.reshape(-1, 8, LANES), 0)

    def d_act_tile(start, lanes):
        window = pl.ds(start, COLS + 2 * PAD)
        cols = pl.ds(start, COLS)
        kernel = [kernel_ref[tap : tap + 1, lanes] for tap in range(9)]
        size = COLS + 2 * PAD
        shifts = (1, 0, size - 1)
        for row in range(rows):
            d_act[row, cols, lanes] = inner(
                row_taps(d_ext, (row, row + 1, row + 2), window, lanes, kernel, True)
            )
        act = [act_mid_ref[row, cols, lanes].astype(F32) for row in range(rows + 2)]
        moved = [
            [inner(pltpu.roll(d_ext[1 + row, window, lanes], shifts[2 - j], 0)) if j != 1
             else inner(d_ext[1 + row, window, lanes]) for j in range(3)]
            for row in range(rows)
        ]
        for i in range(3):
            for j in range(3):
                total = moved[0][j] * act[i]
                for row in range(1, rows):
                    total = total + moved[row][j] * act[i + row]
                sums[3 * i + j, :, lanes] += fold(total)
        up = [up_ext[1 + row, pl.ds(start + PAD, COLS), lanes] for row in range(rows + 2)]
        moved = [
            [inner(pltpu.roll(hid_ext[row, window, lanes], shifts[j], 0)) if j != 1
             else inner(hid_ext[row, window, lanes]) for j in range(3)]
            for row in range(rows)
        ]
        for i in range(3):
            for j in range(3):
                total = moved[0][j] * up[2 - i]
                for row in range(1, rows):
                    total = total + moved[row][j] * up[2 - i + row]
                sums[9 + 3 * i + j, :, lanes] += fold(total)

    for_tiles(width, dim, d_act_tile)

    factor_one, factor_two = factor_ref[0:1, :], factor_ref[1:2, :]
    scale_one = jnp.zeros((1, dim), F32)
    step = 64
    for row in range(rows):
        for part in range(width // step):
            span = slice(row * width + part * step, row * width + (part + 1) * step)
            cols = slice(part * step, (part + 1) * step)
            normed, inverse = norm_stats(residual_ref[span, :].astype(F32))
            d_res = up_ref[row, cols, :].astype(F32) + norm_back(
                d_act[row, cols, :], gain_two_ref[...], normed, inverse
            )
            d_res_ref[span, :] = d_res
            scale_one = scale_one + jnp.sum(projected_ref[span, :] * d_res, 0, keepdims=True)
            d_proj_ref[span, :] = (factor_one * d_res).astype(BF16)
    scale_two = jnp.zeros((1, dim), F32)
    small_ref = prob_out_ref.at[head_dim:]
    small_ref[20:, :] = jnp.zeros((4, dim), F32)
    for tap in range(9):
        small_ref[tap : tap + 1, :] = jnp.sum(sums[tap], 0, keepdims=True)
        raw = jnp.sum(sums[9 + tap], 0, keepdims=True)
        small_ref[9 + tap : 10 + tap, :] = raw * factor_two
        scale_two = scale_two + raw * kernel_ref[9 + tap : 10 + tap, :]
    small_ref[18:19, :] = scale_one
    small_ref[19:20, :] = scale_two
    d_att_ref[...] = dot32(d_proj_ref[...], w_out_ref[...], 1, 1).astype(BF16)
    for block in range(blocks):
        lanes = slice(block * LANES, (block + 1) * LANES)
        prob, *_, block_id, _ = softmax_block(pack_ref, sharp_ref, block, head_dim)
        d_att = d_att_ref[:, lanes]
        prob_out_ref[:head_dim, lanes] = compact(block_id, dot32(d_att, mixed_ref[:, 2 * dim + block * LANES : 2 * dim + (block + 1) * LANES], 0, 0))
        d_value_ref[:, lanes] = dot32(d_att, block_diag(block_id, prob), 1, 0).astype(BF16)
    grad_ref[:, :dim] = dot32(act_one_ref[...], d_value_ref[...], 0, 0).astype(BF16)
    grad_ref[:, dim:] = dot32(attended_ref[...], d_proj_ref[...], 0, 0).astype(BF16)
    split_rows(grad_ref, keep_ref, give_ref, edge_ref[3])


def split_rows(full_ref, keep_ref, give_ref, bit):
    count = keep_ref.shape[0]
    size = keep_ref.shape[1]
    for index in range(count):
        for ref, side in ((keep_ref, bit), (give_ref, 1 - bit)):
            start = pl.multiple_of((2 * index + side) * size, size)
            ref[index] = full_ref[pl.ds(start, size), :]


def gram_kernel(
    edge_ref, sharp_ref, pack_ref, prob_ref, mixed_ref, act_ref, d_qk_ref, keep_ref, give_ref, grad_ref,
):
    _, dim = act_ref.shape
    head_dim = dim // sharp_ref.shape[0]
    for block in range(dim // LANES):
        lanes = slice(block * LANES, (block + 1) * LANES)
        key_lanes = slice(dim + block * LANES, dim + (block + 1) * LANES)
        prob, scores, sharp, divisor, query_col, key_row, block_id, diag = softmax_block(
            pack_ref, sharp_ref, block, head_dim
        )
        prob_grad = prob_ref[:head_dim, lanes]
        d_scores = prob * (prob_grad - seg_sum(block_id, prob * prob_grad))
        d_gram = block_diag(block_id, d_scores * sharp / divisor)
        weighted = d_scores * scores
        d_qsq_col = -seg_sum(block_id, weighted) / (2.0 * query_col * query_col)
        d_qsq = jnp.sum(jnp.where(diag, d_qsq_col, 0.0), 0, keepdims=True)
        d_ksq = -jnp.sum(weighted, 0, keepdims=True) / (2.0 * key_row * key_row)
        query, key = mixed_ref[:, lanes], mixed_ref[:, key_lanes]
        d_query = dot32(key, d_gram, 1, 1) + 2.0 * d_qsq * query.astype(F32)
        d_key = dot32(query, d_gram, 1, 0) + 2.0 * d_ksq * key.astype(F32)
        d_qk_ref[:, lanes] = d_query.astype(BF16)
        d_qk_ref[:, key_lanes] = d_key.astype(BF16)
    act = act_ref[...]
    for part in range(2 * dim // 256):
        cols = slice(part * 256, part * 256 + 256)
        grad_ref[:, cols] = dot32(act, d_qk_ref[:, cols], 0, 0).astype(BF16)
    split_rows(grad_ref, keep_ref, give_ref, edge_ref[3])


def input_kernel(x_ref, gain_ref, w_ref, d_qk_ref, d_value_ref, d_res_ref, out_ref):
    tokens, dim = x_ref.shape
    step = 128
    for part in range(tokens // step):
        rows = slice(part * step, (part + 1) * step)
        d_act = dot32(d_qk_ref[rows, :], w_ref[:, : 2 * dim], 1, 1) + dot32(
            d_value_ref[rows, :], w_ref[:, 2 * dim :], 1, 1
        )
        normed, inverse = norm_stats(x_ref[rows, :].astype(F32))
        out_ref[rows, :] = (
            d_res_ref[rows, :] + norm_back(d_act, gain_ref[...], normed, inverse)
        ).astype(BF16)


def call(body, outs, args, scalars=0, scratch=(), limit=16):
    args = [
        arg if i < scalars else pltpu.with_memory_space_constraint(arg, pltpu.VMEM)
        for i, arg in enumerate(args)
    ]
    specs = [
        pl.BlockSpec(memory_space=pltpu.SMEM if i < scalars else pltpu.VMEM)
        for i in range(len(args))
    ]
    return pl.pallas_call(
        body,
        out_shape=[pltpu.VMEM(shape, dtype) for shape, dtype in outs],
        in_specs=specs,
        out_specs=[pl.BlockSpec(memory_space=pltpu.VMEM)] * len(outs),
        scratch_shapes=[pltpu.VMEM(shape, dtype) for shape, dtype in scratch],
        compiler_params=pltpu.CompilerParams(vmem_limit_bytes=limit << 20),
    )(*args)


def beside(value):
    return swap_bit(value, "sp", 1)


def beyond(value):
    count = lax.axis_size("sp")
    hops = [(i, i - 2) for i in range(count) if i % 2 == 1 and i >= 2]
    hops += [(i, i + 2) for i in range(count) if i % 2 == 0 and i + 2 < count]
    return lax.ppermute(value, "sp", hops)


def after(value, *earlier):
    return lax.optimization_barrier((value, *earlier))[0]


def shards(x4, up4, gain_one, w_qkv, sharp, w_out, factors, gain_two, kernels):
    rows, width, dim = x4.shape[1:]
    heads = sharp.shape[0]
    head_dim = dim // heads
    tokens = rows * width
    x_own, up_own = x4[0], up4[0]
    flat = x_own.reshape(tokens, dim)
    gain_one, gain_two = gain_one[None], gain_two[None]
    taps = kernels.reshape(-1, dim)
    index = lax.axis_index("sp")
    last = lax.axis_size("sp") - 1
    edges = jnp.stack(
        [1 - index % 2, jnp.minimum(index, 1), jnp.minimum(last - index, 1), own_bit("rep", 1)]
    )
    pack_rows = head_dim + 8
    sp_bits = bits_of("sp")
    sp_bits = sp_bits[1:] + sp_bits[:1]

    x_near = beside(x_own)
    mixed, act_one, pack = call(
        functools.partial(first_kernel, head_dim=head_dim),
        [((tokens, 3 * dim), BF16), ((tokens, dim), BF16), ((pack_rows, dim), F32)],
        (flat, gain_one, w_qkv),
    )
    up_near = beside(after(up_own, pack))
    packs = [pack]
    for bit in sp_bits:
        packs.append(packs[-1] + swap_bit(packs[-1], "sp", bit))
    x_far = beyond(after(x_near, packs[1]))
    up_far = beyond(after(up_near, packs[-2]))
    pack = packs[-1]
    attended, projected, residual, act_mid, hidden, slope = call(
        attend_kernel,
        [((tokens, dim), BF16), ((tokens, dim), F32), ((tokens, dim), BF16),
         ((rows + 2, width, dim), BF16), ((rows, width, dim), BF16), ((rows + 2, width, dim), F32)],
        (edges, sharp, pack, x_own, x_near, x_far, mixed, gain_one, gain_two, factors,
         w_qkv, w_out, taps),
        scalars=2,
        scratch=[((rows + 2 * EDGE, width + 2 * PAD, dim), F32), ((dim // LANES, LANES, LANES), BF16)],
    )
    blocks = lax.axis_size("rep")
    split = ((blocks // 2, dim // blocks, 2 * dim), BF16)
    prob_part, d_res, d_value, keep, give = call(
        back_kernel,
        [((head_dim + 24, dim), F32), ((tokens, dim), F32), ((tokens, dim), BF16), split, split],
        (edges, sharp, pack, up_own, up_near, up_far, act_mid, hidden, slope, attended, projected,
         residual, mixed, act_one, gain_two, factors, w_out, taps),
        scalars=2,
        scratch=[((rows + 2 * EDGE, width + 2 * PAD, dim), F32),
                 ((rows + 2, width + 2 * PAD, dim), F32), ((rows, width + 2 * PAD, dim), F32),
                 ((rows, width, dim), F32), ((18, 8, dim), F32), ((tokens, dim), BF16),
                 ((tokens, dim), BF16), ((dim, 2 * dim), BF16)],
    )
    probs = [prob_part]
    for bit in sp_bits:
        probs.append(probs[-1] + swap_bit(probs[-1], "sp", bit))
    prob_part = probs[-1]
    d_qk, late_keep, late_give = call(
        gram_kernel,
        [((tokens, 2 * dim), BF16), split, split],
        (edges, sharp, pack, prob_part, mixed, act_one), scalars=2,
        scratch=[((dim, 2 * dim), BF16)],
    )
    rep_bits = bits_of("rep")

    early = add_low([keep, swap_bit(give, "rep", rep_bits[0])])
    early = rep_rest(early, rep_bits[1:])

    late = add_low([late_keep, swap_bit(late_give, "rep", rep_bits[0])])
    late = rep_rest(late, rep_bits[1:])
    both = jnp.concatenate([late, early], -1)
    both = sp_rows(both)

    small = prob_part[head_dim:]
    small = small + swap_bit(after(small, d_qk), "rep", rep_bits[0])
    for bit in rep_bits[1:]:
        small = small + swap_bit(small, "rep", bit)
    (grad_input,) = call(
        input_kernel, [((tokens, dim), BF16)],
        (flat, gain_one, w_qkv, d_qk, d_value, d_res),
    )
    return (
        grad_input.reshape(1, rows, width, dim),
        both[:, : 3 * dim],
        both[:, 3 * dim :],
        small[:18].reshape(kernels.shape),
        small[18:20],
    )


def solution(mesh):
    rows = P("rep", "sp", None, None)
    return jax.shard_map(
        shards,
        mesh=mesh,
        in_specs=(rows, rows) + (P(),) * 7,
        out_specs=(rows, P("rep", None), P("rep", None), P(), P()),
        check_vma=False,
    )
```
